512 devices in a mesh: member: 4 (over y_hi, core), lat: 8 (over x, y_lo), lon: 16 (over z).
Axes of the slice: x: 4, y: 4 (y_hi: 2, y_lo: 2; y = y_hi * 2 + y_lo), z: 16, core: 2. Of those that a mesh axis runs over, the one named last changes fastest.
Arguments:
- fields: bfloat16 [12, 128, 128, 256], P('member', 'lat', 'lon'), may hold values from -6 to 6
- land_mask: int32 [128, 128], P('lat', 'lon'), may hold values 0 or 1
- offsets: int32 [2], replicated, may hold values from 1 to 7
- land_embed: float32 [256], replicated, may hold values from -5 to 5
- win_qkv: bfloat16 [256, 768], replicated, may hold values from -16 to 16, as said below
- win_out: bfloat16 [256, 256], replicated, may hold values from -0.375 to 0.375
- win_up: bfloat16 [256, 1024], replicated, may hold values from -0.375 to 0.375
- win_down: bfloat16 [1024, 256], replicated, may hold values from -0.1875 to 0.1875
- mem_qkv: bfloat16 [256, 768], replicated, may hold values from -16 to 16, as said below
- mem_out: bfloat16 [256, 256], replicated, may hold values from -0.375 to 0.375
- shift_qkv: bfloat16 [256, 768], replicated, may hold values from -16 to 16, as said below
- shift_out: bfloat16 [256, 256], replicated, may hold values from -0.375 to 0.375
- shift_up: bfloat16 [256, 1024], replicated, may hold values from -0.375 to 0.375
- shift_down: bfloat16 [1024, 256], replicated, may hold values from -0.1875 to 0.1875
Outputs:
- updated: bfloat16 [12, 128, 128, 256], P('member', 'lat', 'lon')
The draws below stay inside these ranges and needn't reach their ends.
Inputs may be any that keep to these rules, and one draw needn't show every extreme that they name: `win_qkv`: query, key and value projection: columns 0 to 255 are queries, then keys, then values, each in 4 heads of 64. `mem_qkv`: laid out as win_qkv. `shift_qkv`: laid out as win_qkv.
All inputs are finite; a program needn't handle non-finite values. No bound on the sum of `land_mask` on one device may be relied on, other than what follows from the above.
Results may differ from the reference program's by a relative error of at most 0.013.
Values may be sent and summed in bfloat16 or wider, within the bound.
A program may use at most 64 MiB of HBM per device.

```python
import math
import jax
import jax.numpy as jnp
from jax import lax

D = 256
HEADS = 4
HID = 1024
WIN = 8
MEMBERS = 12
NLAT = 128
NLON = 128


def attention_weights(key, salt_value):
    key = jax.random.fold_in(key, salt_value)
    base_key = jax.random.fold_in(key, 0)
    matrix = jax.random.truncated_normal(base_key, -4.0, 4.0, (D, 3 * D), jnp.float32) / math.sqrt(D)
    return matrix.astype(jnp.bfloat16)


def draw_win_qkv(key, part):
    return attention_weights(key, 11)


def draw_mem_qkv(key, part):
    return attention_weights(key, 12)


def draw_shift_qkv(key, part):
    return attention_weights(key, 13)


def place_ends(drawn, stream_key, low, top_value):
    longest = drawn.shape.index(max(drawn.shape))
    spots = []
    for shift in (0, 1):
        where = [jax.random.randint(jax.random.fold_in(stream_key, axis), (), 0, length) for axis, length in enumerate(drawn.shape)]
        where[longest] = (where[longest] + shift) % drawn.shape[longest]
        spots.append(tuple(where))
    return drawn.at[spots[0]].set(low).at[spots[1]].set(top_value)


def block_levels(stream_key, extent, cuts, low, top_value):
    def one(position, shards_of):
        draws = jax.random.uniform(jax.random.fold_in(jax.random.fold_in(stream_key, 6), position), (shards_of,), jnp.float32, low / len(cuts), top_value / len(cuts))
        return jnp.repeat(jnp.exp(draws), extent[position] // shards_of).reshape((-1,) + (1,) * (len(extent) - position - 1))

    factor_of = one(*cuts[0])
    for cut in cuts[1:]:
        factor_of = factor_of * one(*cut)
    return factor_of


def bell_draw(stream_key, extent, scale, bound, cuts=(), held_as=jnp.bfloat16):
    array = jax.random.normal(stream_key, extent, jnp.float32) * scale
    if len(cuts) > 0:
        array = block_levels(stream_key, extent, cuts, -0.22, 0.18) * array
    return jnp.clip(array, min=-bound, max=bound).astype(held_as)


def setup_inputs(seed: int = 0) -> dict:
    seeds = jax.random.split(jax.random.key(seed), 15)
    return {
        "fields": bell_draw(seeds[0], (MEMBERS, NLAT, NLON, D), 1.0, 6.0, ((0, 4), (1, 8), (2, 16))),
        "land_mask": place_ends((jax.random.randint(seeds[1], (NLAT, NLON), 0, 10) < 3).astype(jnp.int32), jax.random.fold_in(seeds[1], 1), 0, 1),
        "offsets": jax.random.randint(seeds[2], (2,), 1, WIN).astype(jnp.int32),
        "land_embed": bell_draw(seeds[3], (D,), 1.0, 5.0, (), jnp.float32),
        "win_qkv": draw_win_qkv(jax.random.fold_in(seeds[14], 71), 0),
        "win_out": bell_draw(seeds[5], (D, D), D ** -0.5, 0.375),
        "win_up": bell_draw(seeds[6], (D, HID), D ** -0.5, 0.375),
        "win_down": bell_draw(seeds[7], (HID, D), HID ** -0.5, 0.1875),
        "mem_qkv": draw_mem_qkv(jax.random.fold_in(seeds[14], 71), 0),
        "mem_out": bell_draw(seeds[9], (D, D), D ** -0.5, 0.375),
        "shift_qkv": draw_shift_qkv(jax.random.fold_in(seeds[14], 71), 0),
        "shift_out": bell_draw(seeds[11], (D, D), D ** -0.5, 0.375),
        "shift_up": bell_draw(seeds[12], (D, HID), D ** -0.5, 0.375),
        "shift_down": bell_draw(seeds[13], (HID, D), HID ** -0.5, 0.1875),
    }


epsilon = 1e-05

def normalize(stream):
    average = lax.optimization_barrier(jnp.mean(stream, axis=-1, keepdims=True))
    centered = stream - average
    spread = lax.optimization_barrier(jnp.mean(centered * centered, axis=-1, keepdims=True))
    return (centered * lax.rsqrt(spread + epsilon)).astype(jnp.bfloat16)

def project(inputs, matrix):
    flattened = inputs.reshape(-1, inputs.shape[-1])
    result = jnp.dot(flattened, matrix, preferred_element_type=jnp.float32)
    return result.reshape(inputs.shape[:-1] + (matrix.shape[1],))

def to_windows(tensor):
    height, breadth, channels = tensor.shape
    tensor = tensor.reshape(height // WIN, WIN, breadth // WIN, WIN, channels)
    return tensor.transpose(0, 2, 1, 3, 4).reshape(height // WIN, breadth // WIN, WIN * WIN, channels)

def from_windows(tensor, height, breadth):
    channels = tensor.shape[-1]
    tensor = tensor.reshape(height // WIN, breadth // WIN, WIN, WIN, channels).transpose(0, 2, 1, 3, 4)
    return tensor.reshape(height, breadth, channels)

def window_attention(qkv_rows, window_tag):
    height, breadth, triple = qkv_rows.shape
    channels = triple // 3
    head_size = channels // HEADS
    blocks = to_windows(qkv_rows)
    split_heads = blocks.reshape(blocks.shape[:3] + (3, HEADS, head_size)).astype(jnp.float32)
    scores = jnp.einsum('abqhe,abkhe->abhqk', split_heads[:, :, :, 0], split_heads[:, :, :, 1]) * head_size ** (-0.5)
    labels = to_windows(window_tag[:, :, None])[..., 0]
    matched = labels[:, :, :, None] == labels[:, :, None, :]
    scores = jnp.where(matched[:, :, None], scores, -1e+30)
    weights = jax.nn.softmax(scores, axis=-1).astype(jnp.bfloat16)
    result = jnp.einsum('abhqk,abkhe->abqhe', weights.astype(jnp.float32), split_heads[:, :, :, 2])
    result = result.astype(jnp.bfloat16).reshape(blocks.shape[:3] + (channels,))
    return from_windows(result, height, breadth)

def window_block(stream, window_tag, w_qkv, w_out, w_up, w_down):
    qkv_rows = project(normalize(stream), w_qkv).astype(jnp.bfloat16)
    stream = stream + project(window_attention(qkv_rows, window_tag), w_out)
    hidden = jax.nn.gelu(project(normalize(stream), w_up), approximate=False).astype(jnp.bfloat16)
    return stream + project(hidden, w_down)

def member_block(stream, w_qkv, w_out):
    members, breadth, channels = stream.shape
    head_size = channels // HEADS
    qkv_rows = project(normalize(stream), w_qkv).astype(jnp.bfloat16)
    split_heads = qkv_rows.reshape(members, breadth, 3, HEADS, head_size).astype(jnp.float32)
    scores = jnp.einsum('mthe,nthe->thmn', split_heads[:, :, 0], split_heads[:, :, 1]) * head_size ** (-0.5)
    weights = jax.nn.softmax(scores, axis=-1).astype(jnp.bfloat16)
    result = jnp.einsum('thmn,nthe->mthe', weights.astype(jnp.float32), split_heads[:, :, 2])
    result = result.astype(jnp.bfloat16).reshape(members, breadth, channels)
    return stream + project(result, w_out)

def reference(fields, land_mask, offsets, land_embed, win_qkv, win_out, win_up, win_down, mem_qkv, mem_out, shift_qkv, shift_out, shift_up, shift_down):
    stream = fields.astype(jnp.float32) + land_mask.astype(jnp.float32)[None, :, :, None] * land_embed[None, None, None, :]
    no_groups = jnp.zeros((NLAT, NLON), jnp.int32)
    stream = lax.map(lambda member: window_block(member, no_groups, win_qkv, win_out, win_up, win_down), stream)
    stream = lax.map(lambda lat_row: member_block(lat_row, mem_qkv, mem_out), stream.transpose(1, 0, 2, 3)).transpose(1, 0, 2, 3)
    wrapped = ((jnp.arange(NLAT, dtype=jnp.int32) + offsets[0]) % NLAT < offsets[0]).astype(jnp.int32)
    window_tag = jnp.broadcast_to(wrapped[:, None], (NLAT, NLON))

    def shifted(member):
        rolled = jnp.roll(member, (-offsets[0], -offsets[1]), axis=(0, 1))
        finished = window_block(rolled, window_tag, shift_qkv, shift_out, shift_up, shift_down)
        return jnp.roll(finished, (offsets[0], offsets[1]), axis=(0, 1))
    stream = lax.map(shifted, stream)
    return stream.astype(jnp.bfloat16)
```

```python
import functools

import jax
import jax.numpy as jnp
from jax import lax
from jax.experimental import pallas as pl
from jax.experimental.pallas import tpu as pltpu
from jax.sharding import PartitionSpec as P

HEADS = 4
WIN = 8
EPS = 1e-05
NEG = -1e30
MESH = pl.DeviceIdType.MESH
BF = jnp.bfloat16
F32 = jnp.float32


def normalize(stream):
    average = jnp.mean(stream, axis=-1, keepdims=True)
    centered = stream - average
    spread = jnp.mean(centered * centered, axis=-1, keepdims=True)
    return (centered * lax.rsqrt(spread + EPS)).astype(BF)


def project(inputs, matrix):
    return jnp.dot(inputs, matrix, preferred_element_type=F32)


def gelu(x):
    return (0.5 * x) * (1.0 + lax.erf(x * 0.7071067811865476))


def feed_forward(stream, w_up, w_down):
    hidden = gelu(project(normalize(stream), w_up)).astype(BF)
    return stream + project(hidden, w_down)


def head_masks(channels, dtype):
    lane = lax.broadcasted_iota(jnp.int32, (1, channels), 1) // (channels // HEADS)
    return [jnp.where(lane == h, 1.0, 0.0).astype(dtype) for h in range(HEADS)]


def attend(q, k, v, bias, masks_bf, masks_f32):
    count = q.shape[0]
    stacked = jnp.concatenate([q * mask for mask in masks_bf], axis=0)
    scores = lax.dot_general(
        stacked, k, (((1,), (1,)), ((), ())), preferred_element_type=F32
    )
    if bias is not None:
        scores = (
            scores.reshape(HEADS, count, -1) + bias[None]
        ).reshape(scores.shape)
    top = jnp.max(scores, axis=-1, keepdims=True)
    weights = jnp.exp(scores - top)
    total = jnp.sum(weights, axis=-1, keepdims=True)
    weights = (weights * (1.0 / total)).astype(BF)
    wide = project(weights, v)
    result = wide[:count] * masks_f32[0]
    for h in range(1, HEADS):
        result = result + wide[h * count : (h + 1) * count] * masks_f32[h]
    return result


def kernel(
    sizes,
    fields, land, offsets, embed,
    h_win_qkv, h_win_out, h_win_up, h_win_down, h_mem_qkv, h_mem_out,
    h_shift_qkv, h_shift_out, h_shift_up, h_shift_down,
    out,
    win_qkv, win_out, win_up, win_down, mem_qkv, mem_out,
    shift_qkv, shift_out, shift_up, shift_down,
    stream, mine, got, qkv, mixed, mixed_send, mixed_got,
    late, vert, left, right, corner, corner_left, corner_right,
    biases,
    w_sem, a_send, a_recv, r_send, r_recv, v_send, v_recv,
    l_send, l_recv, rt_send, rt_recv, c_send, c_recv,
):
    n_member, n_lat, n_lon = sizes
    members = fields.shape[0]
    channels = fields.shape[-1]
    tokens = WIN * WIN
    me = lax.axis_index("member")
    lat = lax.axis_index("lat")
    lon = lax.axis_index("lon")
    core = lax.rem(me, 2)
    chip = me // 2
    other = 1 - core
    mate = {"member": 2 * chip + other}
    far_same = {"member": 2 * (1 - chip) + core}
    far_other = {"member": 2 * (1 - chip) + other}
    lat_up = {"lat": lax.rem(lat + n_lat - 1, n_lat)}
    lat_down = {"lat": lax.rem(lat + 1, n_lat)}
    lon_left = {"lon": lax.rem(lon + n_lon - 1, n_lon)}
    lon_right = {"lon": lax.rem(lon + 1, n_lon)}

    barrier = pltpu.get_barrier_semaphore()
    for peer in (mate, far_same, far_other, lat_up, lat_down, lon_left, lon_right):
        pl.semaphore_signal(barrier, inc=1, device_id=peer, device_id_type=MESH)

    pairs = [
        (h_win_qkv, win_qkv), (h_win_out, win_out), (h_win_up, win_up),
        (h_win_down, win_down), (h_mem_qkv, mem_qkv), (h_mem_out, mem_out),
        (h_shift_qkv, shift_qkv), (h_shift_out, shift_out),
        (h_shift_up, shift_up), (h_shift_down, shift_down),
    ]
    loads = [
        pltpu.make_async_copy(source, target, w_sem.at[i])
        for i, (source, target) in enumerate(pairs)
    ]
    for load in loads:
        load.start()

    off0 = offsets[0]
    off1 = offsets[1]
    split0 = WIN - off0
    split1 = WIN - off1
    masks_bf = head_masks(channels, BF)
    masks_f32 = head_masks(channels, F32)
    scale = (channels // HEADS) ** -0.5

    def push(source, target, send, recv, peer):
        copy = pltpu.make_async_remote_copy(
            src_ref=source, dst_ref=target, send_sem=send, recv_sem=recv,
            device_id=peer, device_id_type=MESH,
        )
        copy.start()
        return copy

    token = lax.broadcasted_iota(jnp.int32, (tokens, channels), 0)
    row_low = jnp.where(token // WIN < split0, 1.0, 0.0)
    col_low = jnp.where(lax.rem(token, WIN) < split1, 1.0, 0.0)
    mr, nr = row_low.astype(BF), (1.0 - row_low).astype(BF)
    mc, nc = col_low.astype(BF), (1.0 - col_low).astype(BF)
    q_tok = lax.broadcasted_iota(jnp.int32, (tokens, 4 * tokens), 0)
    k_tok = lax.broadcasted_iota(jnp.int32, (tokens, 4 * tokens), 1)
    q_row = jnp.where(q_tok // WIN < split0, 1, 0)
    q_col = jnp.where(lax.rem(q_tok, WIN) < split1, 1, 0)
    k_row = k_tok // (2 * tokens)
    k_col = lax.rem(k_tok // tokens, 2)
    k_low = jnp.where(lax.rem(k_tok, tokens) // WIN < split0, 1, 0)
    wrong = jnp.where(q_row == k_row, 0.0, NEG) + jnp.where(q_col == k_col, 0.0, NEG)
    first = jnp.where(lat == 0, 1.0, 0.0)
    last = jnp.where(lat == n_lat - 1, 1.0, 0.0)
    outside0 = jnp.where(k_row == 0, jnp.where(k_low == 1, NEG, 0.0), 0.0) * first
    outside1 = jnp.where(k_row == 1, jnp.where(k_low == 0, NEG, 0.0), 0.0) * last
    biases[0] = wrong + outside0
    biases[1] = wrong + outside1

    def window_block(block):
        s_row = lax.broadcasted_iota(jnp.int32, (tokens, WIN), 0)
        s_lane = lax.broadcasted_iota(jnp.int32, (tokens, WIN), 1)
        rows = [WIN * block + lax.rem(s + off0, WIN) for s in range(WIN)]
        spread = jnp.concatenate(
            [jnp.broadcast_to(land[pl.ds(r, 1), :], (WIN, WIN)) for r in rows], axis=0
        )
        picked = jnp.where(
            s_lane == lax.rem(lax.rem(s_row, WIN) + off1, WIN), spread.astype(F32), 0.0
        )
        is_land = jnp.sum(picked, axis=-1, keepdims=True)
        added = is_land * embed[...]
        parts = []
        for m in range(members):
            tile = jnp.concatenate(
                [fields[m, r].astype(F32).reshape(1, WIN, channels) for r in rows], axis=0
            )
            tile = pltpu.roll(tile, split1, 1)
            parts.append(tile.reshape(tokens, channels) + added)
        x = jnp.concatenate(parts, axis=0)
        return x

    def window_section(block, waits):
        x = window_block(block)
        if waits:
            loads[0].wait()
        proj = project(normalize(x), win_qkv[...])
        atts = []
        for m in range(members):
            rows = slice(m * tokens, (m + 1) * tokens)
            q = (proj[rows, :channels] * scale).astype(BF)
            k = proj[rows, channels : 2 * channels].astype(BF)
            v = proj[rows, 2 * channels :].astype(BF)
            atts.append(attend(q, k, v, None, masks_bf, masks_f32))
        if waits:
            loads[1].wait()
        x = x + project(jnp.concatenate(atts, axis=0).astype(BF), win_out[...])
        if waits:
            loads[2].wait()
            loads[3].wait()
        x = feed_forward(x, win_up[...], win_down[...])
        stream[block] = x.reshape(members, WIN, WIN, channels)
        mine[block] = normalize(x).reshape(members, tokens, channels)

    window_section(other, True)
    pl.semaphore_wait(barrier, 7)
    sends = [
        push(mine.at[other], got.at[2], a_send.at[2], a_recv.at[2], far_other),
        push(mine.at[other], got.at[0], a_send.at[0], a_recv.at[0], mate),
    ]
    window_section(core, False)
    sends.append(push(mine.at[core], got.at[1], a_send.at[1], a_recv.at[1], far_same))

    loads[4].wait()

    def member_qkv(source, x, with_q):
        weights = mem_qkv[...] if with_q else mem_qkv[:, channels:]
        first_col = 0 if with_q else channels
        qkv[source, :, :, first_col:] = project(
            x.reshape(members * tokens, channels), weights
        ).reshape(members, tokens, -1)

    member_qkv(0, mine[core], True)
    sends[1].wait_recv()
    member_qkv(1, got[0], True)
    sends[0].wait_recv()
    member_qkv(2, got[2], False)
    sends[2].wait_recv()
    member_qkv(3, got[1], False)

    near = 2 * members
    total = 4 * members
    qt = lax.rem(lax.broadcasted_iota(jnp.int32, (near * WIN, total * WIN), 0), WIN)
    kt = lax.rem(lax.broadcasted_iota(jnp.int32, (near * WIN, total * WIN), 1), WIN)
    same_token = jnp.where(qt == kt, 0.0, NEG)
    for group in range(tokens // WIN):
        span = slice(group * WIN, (group + 1) * WIN)
        q = qkv[0:2, :, span, 0:channels].reshape(near * WIN, channels)
        k = qkv[:, :, span, channels : 2 * channels].reshape(total * WIN, channels)
        v = qkv[:, :, span, 2 * channels :].reshape(total * WIN, channels)
        att = attend(
            (q * scale).astype(BF), k.astype(BF), v.astype(BF), same_token,
            masks_bf, masks_f32,
        )
        mixed[:, :, span, :] = att.reshape(2, members, WIN, channels)
    mixed_send[...] = mixed[1].astype(BF)
    back = push(mixed_send, mixed_got, r_send, r_recv, mate)
    loads[5].wait()

    def member_add(block, att):
        x = stream[block].reshape(members * tokens, channels)
        x = x + project(att, mem_out[...])
        stream[block] = x.reshape(members, WIN, WIN, channels)
        late[block] = normalize(x).reshape(members, tokens, channels)

    halo = []

    def send_halo(block):
        toward = {"lat": lax.rem(lat + 2 * block - 1 + n_lat, n_lat)}
        for m in range(members):
            piece = late.at[block, m]
            halo.append(
                push(piece, vert.at[1 - block, m], v_send.at[block, m],
                     v_recv.at[1 - block, m], toward)
            )
            halo.append(
                push(piece, right.at[block, m], l_send.at[block, m],
                     l_recv.at[block, m], lon_left)
            )
            halo.append(
                push(piece, left.at[block, m], rt_send.at[block, m],
                     rt_recv.at[block, m], lon_right)
            )

    member_add(core, mixed[0].reshape(members * tokens, channels).astype(BF))
    send_halo(core)
    back.wait_recv()
    member_add(other, mixed_got[...].reshape(members * tokens, channels))
    send_halo(other)

    def arrived(buffer, sem):
        pltpu.make_async_copy(buffer, buffer, sem).wait()

    corners = []
    for m in range(members):
        arrived(vert.at[0, m], v_recv.at[0, m])
        arrived(vert.at[1, m], v_recv.at[1, m])
        corner[m] = vert[0, m] * mr + vert[1, m] * nr
        corners.append(
            push(corner.at[m], corner_right.at[m], c_send.at[0, m], c_recv.at[0, m], lon_left)
        )
        corners.append(
            push(corner.at[m], corner_left.at[m], c_send.at[1, m], c_recv.at[1, m], lon_right)
        )

    for load in loads[6:]:
        load.wait()

    for m in range(members):
        for block in range(2):
            arrived(right.at[block, m], l_recv.at[block, m])
            arrived(left.at[block, m], rt_recv.at[block, m])
        arrived(corner_right.at[m], c_recv.at[0, m])
        arrived(corner_left.at[m], c_recv.at[1, m])
        own = [late[0, m], late[1, m]]
        edge = corner[m]
        side = [left[b, m] * mc + right[b, m] * nc for b in range(2)]
        far = corner_left[m] * mc + corner_right[m] * nc
        middle = [edge * mr + own[0] * nr, own[0] * mr + own[1] * nr, own[1] * mr + edge * nr]
        flank = [far * mr + side[0] * nr, side[0] * mr + side[1] * nr, side[1] * mr + far * nr]
        windows = []
        for g in range(3):
            windows.append(flank[g] * mc + middle[g] * nc)
            windows.append(middle[g] * mc + flank[g] * nc)
        keyed = project(jnp.concatenate(windows, axis=0), shift_qkv[:, channels:]).astype(BF)
        asked = project(jnp.concatenate(own, axis=0), shift_qkv[:, :channels])
        asked = (asked * scale).astype(BF)
        atts = []
        for b in range(2):
            keys = slice(2 * tokens * b, 2 * tokens * b + 4 * tokens)
            atts.append(
                attend(
                    asked[b * tokens : (b + 1) * tokens], keyed[keys, :channels],
                    keyed[keys, channels:], biases[b], masks_bf, masks_f32,
                )
            )
        x = jnp.concatenate(
            [stream[b, m].reshape(tokens, channels) for b in range(2)], axis=0
        )
        x = x + project(jnp.concatenate(atts, axis=0).astype(BF), shift_out[...])
        x = feed_forward(x, shift_up[...], shift_down[...])
        for b in range(2):
            stream[b, m] = x[b * tokens : (b + 1) * tokens].reshape(WIN, WIN, channels)
        for b in range(2):
            tile = jnp.concatenate(
                [
                    stream[b, m, lax.rem(r + split0, WIN)].reshape(1, WIN, channels)
                    for r in range(WIN)
                ],
                axis=0,
            )
            tile = pltpu.roll(tile, off1, 1)
            out[m, b * WIN : (b + 1) * WIN] = tile.astype(BF)

    for copy in sends + [back] + halo + corners:
        copy.wait_send()


def per_device(sizes, fields, land_mask, offsets, land_embed, *weights):
    members, height, breadth, channels = fields.shape
    tokens = WIN * WIN
    vmem = pl.BlockSpec(memory_space=pltpu.VMEM)
    tile = (members, tokens, channels)
    dma = pltpu.SemaphoreType.DMA
    scratch = [pltpu.VMEM(w.shape, w.dtype) for w in weights] + [
        pltpu.VMEM((2, members, WIN, WIN, channels), F32),
        pltpu.VMEM((2,) + tile, BF),
        pltpu.VMEM((3,) + tile, BF),
        pltpu.VMEM((4, members, tokens, 3 * channels), F32),
        pltpu.VMEM((2,) + tile, F32),
        pltpu.VMEM(tile, BF),
        pltpu.VMEM(tile, BF),
        pltpu.VMEM((2,) + tile, BF),
        pltpu.VMEM((2,) + tile, BF),
        pltpu.VMEM((2,) + tile, BF),
        pltpu.VMEM((2,) + tile, BF),
        pltpu.VMEM(tile, BF),
        pltpu.VMEM(tile, BF),
        pltpu.VMEM(tile, BF),
        pltpu.VMEM((2, tokens, 4 * tokens), F32),
        dma((len(weights),)),
        dma((3,)), dma((3,)), dma, dma,
        dma((2, members)), dma((2, members)),
        dma((2, members)), dma((2, members)),
        dma((2, members)), dma((2, members)),
        dma((2, members)), dma((2, members)),
    ]
    return pl.pallas_call(
        functools.partial(kernel, sizes),
        out_shape=jax.ShapeDtypeStruct(fields.shape, BF),
        in_specs=[vmem, vmem, pl.BlockSpec(memory_space=pltpu.SMEM), vmem]
        + [pl.BlockSpec(memory_space=pl.ANY)] * len(weights),
        out_specs=vmem,
        scratch_shapes=scratch,
        compiler_params=pltpu.CompilerParams(collective_id=0, has_side_effects=True),
        name="scorer",
    )(fields, land_mask, offsets, land_embed.reshape(1, channels), *weights)


def solution(mesh):
    sizes = tuple(mesh.shape[axis] for axis in ("member", "lat", "lon"))
    return jax.shard_map(
        functools.partial(per_device, sizes),
        mesh=mesh,
        in_specs=(P("member", "lat", "lon", None), P("lat", "lon")) + (P(),) * 12,
        out_specs=P("member", "lat", "lon", None),
        check_vma=False,
    )
```

```python
import functools

import jax
import jax.numpy as jnp
from jax import lax
from jax.experimental import pallas as pl
from jax.experimental.pallas import tpu as pltpu
from jax.sharding import PartitionSpec as P

HEADS = 4
WIN = 8
EPS = 1e-05
VMEM_LIMIT = 58 * 1024 * 1024
NEG = -1e30
MESH = pl.DeviceIdType.MESH
BF = jnp.bfloat16
F32 = jnp.float32


def normalize(stream):
    average = jnp.mean(stream, axis=-1, keepdims=True)
    centered = stream - average
    spread = jnp.mean(centered * centered, axis=-1, keepdims=True)
    return (centered * lax.rsqrt(spread + EPS)).astype(BF)


def project(inputs, matrix):
    return jnp.dot(inputs, matrix, preferred_element_type=F32)


def gelu(x):
    return (0.5 * x) * (1.0 + lax.erf(x * 0.7071067811865476))


def feed_forward(stream, w_up, w_down):
    hidden = gelu(project(normalize(stream), w_up)).astype(BF)
    return stream + project(hidden, w_down)


def head_masks(channels, dtype):
    lane = lax.broadcasted_iota(jnp.int32, (1, channels), 1) // (channels // HEADS)
    return [jnp.where(lane == h, 1.0, 0.0).astype(dtype) for h in range(HEADS)]


def attend(q, k, v, bias, masks_bf, masks_f32):
    count = q.shape[0]
    stacked = jnp.concatenate([q * mask for mask in masks_bf], axis=0)
    scores = lax.dot_general(
        stacked, k, (((1,), (1,)), ((), ())), preferred_element_type=F32
    )
    if bias is not None:
        scores = (
            scores.reshape(HEADS, count, -1) + bias[None]
        ).reshape(scores.shape)
    top = jnp.max(scores, axis=-1, keepdims=True)
    weights = jnp.exp(scores - top)
    total = jnp.sum(weights, axis=-1, keepdims=True)
    weights = (weights * (1.0 / total)).astype(BF)
    wide = project(weights, v)
    result = wide[:count] * masks_f32[0]
    for h in range(1, HEADS):
        result = result + wide[h * count : (h + 1) * count] * masks_f32[h]
    return result


def kernel(
    sizes,
    h_fields, land, offsets, embed,
    h_win_qkv, h_win_out, h_win_up, h_win_down, h_mem_qkv, h_mem_out,
    h_shift_qkv, h_shift_out, h_shift_up, h_shift_down,
    out,
    fields, win_qkv, win_out, win_up, win_down, mem_qkv, mem_out,
    shift_qkv, shift_out, shift_up, shift_down,
    stream, mine, got, qkv, mixed, mixed_send, mixed_got,
    late, vert, left, right, corner, corner_left, corner_right,
    w_sem, a_send, a_recv, r_send, r_recv, v_send, v_recv,
    l_send, l_recv, rt_send, rt_recv, c_send, c_recv,
):
    n_member, n_lat, n_lon = sizes
    members = h_fields.shape[0]
    channels = h_fields.shape[-1]
    tokens = WIN * WIN
    part = tokens // 2
    edge, inner = 0, 1
    me = lax.axis_index("member")
    lat = lax.axis_index("lat")
    lon = lax.axis_index("lon")
    core = lax.rem(me, 2)
    chip = me // 2
    other = 1 - core
    mate = {"member": 2 * chip + other}
    far_same = {"member": 2 * (1 - chip) + core}
    far_other = {"member": 2 * (1 - chip) + other}
    lat_up = {"lat": lax.rem(lat + n_lat - 1, n_lat)}
    lat_down = {"lat": lax.rem(lat + 1, n_lat)}
    lon_left = {"lon": lax.rem(lon + n_lon - 1, n_lon)}
    lon_right = {"lon": lax.rem(lon + 1, n_lon)}

    barrier = pltpu.get_barrier_semaphore()
    for peer in (mate, far_same, far_other, lat_up, lat_down, lon_left, lon_right):
        pl.semaphore_signal(barrier, inc=1, device_id=peer, device_id_type=MESH)

    pairs = [
        (h_fields, fields),
        (h_win_qkv, win_qkv), (h_win_out, win_out), (h_win_up, win_up),
        (h_win_down, win_down), (h_mem_qkv, mem_qkv), (h_mem_out, mem_out),
        (h_shift_qkv, shift_qkv), (h_shift_out, shift_out),
        (h_shift_up, shift_up), (h_shift_down, shift_down),
    ]
    loads = [
        pltpu.make_async_copy(source, target, w_sem.at[i])
        for i, (source, target) in enumerate(pairs)
    ]
    for load in loads:
        load.start()

    off0 = offsets[0]
    off1 = offsets[1]
    split0 = WIN - off0
    split1 = WIN - off1
    masks_bf = head_masks(channels, BF)
    masks_f32 = head_masks(channels, F32)
    scale = (channels // HEADS) ** -0.5

    def push(source, target, send, recv, peer):
        copy = pltpu.make_async_remote_copy(
            src_ref=source, dst_ref=target, send_sem=send, recv_sem=recv,
            device_id=peer, device_id_type=MESH,
        )
        copy.start()
        return copy

    token = lax.broadcasted_iota(jnp.int32, (tokens, channels), 0)
    is_low = token // WIN < split0
    row_low = jnp.where(is_low, 1.0, 0.0)
    col_low = jnp.where(lax.rem(token, WIN) < split1, 1.0, 0.0)

    flags = pltpu.roll(land[...].astype(F32), split1, 0)
    spread = jnp.concatenate([flags] * (2 * WIN), axis=0)
    s_row = lax.broadcasted_iota(jnp.int32, spread.shape, 0) // WIN
    s_lane = lax.broadcasted_iota(jnp.int32, spread.shape, 1)
    s_pick = WIN * (s_row // WIN) + lax.rem(lax.rem(s_row, WIN) + off0, WIN)
    is_land = jnp.sum(jnp.where(s_lane == s_pick, spread, 0.0), axis=-1, keepdims=True)
    added = is_land * embed[...]
    rows = [WIN * b + lax.rem(s + off0, WIN) for b in range(2) for s in range(WIN)]

    loads[0].wait()

    def window_section(m):
        tile = jnp.concatenate(
            [fields[m, r].astype(F32).reshape(1, WIN, channels) for r in rows], axis=0
        )
        x = pltpu.roll(tile, split1, 1).reshape(2 * tokens, channels) + added
        if m == 0:
            loads[1].wait()
        proj = project(normalize(x), win_qkv[...])
        atts = []
        for b in range(2):
            span = slice(b * tokens, (b + 1) * tokens)
            q = (proj[span, :channels] * scale).astype(BF)
            k = proj[span, channels : 2 * channels].astype(BF)
            v = proj[span, 2 * channels :].astype(BF)
            atts.append(attend(q, k, v, None, masks_bf, masks_f32))
        if m == 0:
            loads[2].wait()
        x = x + project(jnp.concatenate(atts, axis=0).astype(BF), win_out[...])
        if m == 0:
            loads[3].wait()
            loads[4].wait()
        x = feed_forward(x, win_up[...], win_down[...])
        top, bottom = x[:tokens], x[tokens:]
        tiles = [jnp.where(is_low, bottom, top), jnp.where(is_low, top, bottom)]
        for e in range(2):
            normed = normalize(tiles[e])
            for half in range(2):
                span = slice(half * part, (half + 1) * part)
                stream[e, half, m] = tiles[e][span].reshape(WIN // 2, WIN, channels)
                mine[e, half, m] = normed[span]

    sends = {}

    def send_members(e, m):
        for i, (half, peer) in enumerate(
            ((other, mate), (other, far_other), (core, far_same))
        ):
            sends[i, e, m] = push(
                mine.at[e, half, m], got.at[i, e, m], a_send.at[i, e, m],
                a_recv.at[i, e, m], peer,
            )

    window_section(0)
    pl.semaphore_wait(barrier, 7)
    send_members(edge, 0)
    window_section(1)
    send_members(edge, 1)
    send_members(inner, 0)
    window_section(2)
    send_members(edge, 2)
    send_members(inner, 1)
    send_members(inner, 2)

    near = 2 * members
    total = 4 * members
    qt = lax.rem(lax.broadcasted_iota(jnp.int32, (near * WIN, total * WIN), 0), WIN)
    kt = lax.rem(lax.broadcasted_iota(jnp.int32, (near * WIN, total * WIN), 1), WIN)
    same_token = jnp.where(qt == kt, 0.0, NEG)
    backs = []

    def member_qkv(source, x, with_q):
        weights = mem_qkv[...] if with_q else mem_qkv[:, channels:]
        first_col = 0 if with_q else channels
        qkv[source, :, :, first_col:] = project(
            x.reshape(members * part, channels), weights
        ).reshape(members, part, -1)

    def member_attention(e):
        member_qkv(0, mine[e, core], True)
        for m in range(members):
            sends[0, e, m].wait_recv()
        member_qkv(1, got[0, e], True)
        for i in (1, 2):
            for m in range(members):
                sends[i, e, m].wait_recv()
            member_qkv(i + 1, got[i, e], False)
        for group in range(part // WIN):
            span = slice(group * WIN, (group + 1) * WIN)
            q = qkv[0:2, :, span, 0:channels].reshape(near * WIN, channels)
            k = qkv[:, :, span, channels : 2 * channels].reshape(total * WIN, channels)
            v = qkv[:, :, span, 2 * channels :].reshape(total * WIN, channels)
            att = attend(
                (q * scale).astype(BF), k.astype(BF), v.astype(BF), same_token,
                masks_bf, masks_f32,
            )
            mixed[:, :, span, :] = att.reshape(2, members, WIN, channels)
        mixed_send[e] = mixed[1].astype(BF)
        backs.append(
            push(mixed_send.at[e], mixed_got.at[e], r_send.at[e], r_recv.at[e], mate)
        )

    def member_add(e, half, att):
        x = stream[e, half].reshape(members * part, channels)
        x = x + project(att.reshape(members * part, channels), mem_out[...])
        stream[e, half] = x.reshape(members, WIN // 2, WIN, channels)
        late[e, half] = normalize(x).reshape(members, part, channels)

    halo = []

    def send_lat(half):
        piece = late.at[edge, half]
        halo.append(push(piece, vert.at[1, half], v_send.at[1, half], v_recv.at[1, half], lat_up))
        halo.append(push(piece, vert.at[0, half], v_send.at[0, half], v_recv.at[0, half], lat_down))

    def send_lon(e, half):
        piece = late.at[e, half]
        halo.append(push(piece, right.at[e, half], l_send.at[e, half], l_recv.at[e, half], lon_left))
        halo.append(push(piece, left.at[e, half], rt_send.at[e, half], rt_recv.at[e, half], lon_right))

    def arrived(buffer, sem):
        pltpu.make_async_copy(buffer, buffer, sem).wait()

    loads[5].wait()
    loads[6].wait()
    member_attention(edge)
    member_add(edge, core, mixed[0].astype(BF))
    send_lat(core)
    send_lon(edge, core)
    arrived(mixed_got.at[edge], r_recv.at[edge])
    member_add(edge, other, mixed_got[edge])
    send_lat(other)
    send_lon(edge, other)
    member_attention(inner)
    member_add(inner, core, mixed[0].astype(BF))
    send_lon(inner, core)
    arrived(mixed_got.at[inner], r_recv.at[inner])
    member_add(inner, other, mixed_got[inner])
    send_lon(inner, other)

    mr, nr = row_low.astype(BF), (1.0 - row_low).astype(BF)
    mc, nc = col_low.astype(BF), (1.0 - col_low).astype(BF)
    for half in (core, other):
        arrived(vert.at[0, half], v_recv.at[0, half])
        arrived(vert.at[1, half], v_recv.at[1, half])
        h_tok = lax.broadcasted_iota(jnp.int32, (part, channels), 0) + half * part
        h_low = jnp.where(h_tok // WIN < split0, 1.0, 0.0)
        h_mr, h_nr = h_low.astype(BF), (1.0 - h_low).astype(BF)
        corner[half] = vert[0, half] * h_mr[None] + vert[1, half] * h_nr[None]
        halo.append(
            push(corner.at[half], corner_right.at[half], c_send.at[0, half],
                 c_recv.at[0, half], lon_left)
        )
        halo.append(
            push(corner.at[half], corner_left.at[half], c_send.at[1, half],
                 c_recv.at[1, half], lon_right)
        )

    q_tok = lax.broadcasted_iota(jnp.int32, (tokens, 4 * tokens), 0)
    k_tok = lax.broadcasted_iota(jnp.int32, (tokens, 4 * tokens), 1)
    q_row = jnp.where(q_tok // WIN < split0, 1, 0)
    q_col = jnp.where(lax.rem(q_tok, WIN) < split1, 1, 0)
    k_row = k_tok // (2 * tokens)
    k_col = lax.rem(k_tok // tokens, 2)
    k_low = jnp.where(lax.rem(k_tok, tokens) // WIN < split0, 1, 0)
    col_bias = jnp.where(q_col == k_col, 0.0, NEG)
    first = jnp.where(lat == 0, 1.0, 0.0)
    last = jnp.where(lat == n_lat - 1, 1.0, 0.0)
    outside = jnp.where(k_row == 0, jnp.where(k_low == 1, NEG, 0.0), 0.0) * first
    outside = outside + jnp.where(k_row == 1, jnp.where(k_low == 0, NEG, 0.0), 0.0) * last
    edge_bias = jnp.where(q_row == k_row, 0.0, NEG) + col_bias + outside
    inner_bias = col_bias[:, : 2 * tokens]

    for load in loads[7:]:
        load.wait()

    def whole(ref, m):
        return ref[:, m].reshape(tokens, channels)

    def finish(e, windows, bias):
        count = len(windows[0]) * tokens
        own = jnp.concatenate([whole(late.at[e], m) for m in range(members)], axis=0)
        asked = (project(own, shift_qkv[:, :channels]) * scale).astype(BF)
        keyed = project(
            jnp.concatenate([w for group in windows for w in group], axis=0),
            shift_qkv[:, channels:],
        ).astype(BF)
        atts = []
        for m in range(members):
            keys = slice(m * count, (m + 1) * count)
            atts.append(
                attend(
                    asked[m * tokens : (m + 1) * tokens], keyed[keys, :channels],
                    keyed[keys, channels:], bias, masks_bf, masks_f32,
                )
            )
        x = jnp.concatenate(
            [stream[e, :, m].reshape(tokens, channels) for m in range(members)], axis=0
        )
        x = x + project(jnp.concatenate(atts, axis=0).astype(BF), shift_out[...])
        x = feed_forward(x, shift_up[...], shift_down[...])
        for m in range(members):
            stream[e, :, m] = x[m * tokens : (m + 1) * tokens].reshape(
                2, WIN // 2, WIN, channels
            )

    for half in range(2):
        arrived(right.at[inner, half], l_recv.at[inner, half])
        arrived(left.at[inner, half], rt_recv.at[inner, half])
    windows = []
    for m in range(members):
        own = whole(late.at[inner], m)
        windows.append(
            [
                whole(left.at[inner], m) * mc + own * nc,
                own * mc + whole(right.at[inner], m) * nc,
            ]
        )
    finish(inner, windows, inner_bias)

    for half in range(2):
        arrived(right.at[edge, half], l_recv.at[edge, half])
        arrived(left.at[edge, half], rt_recv.at[edge, half])
    for half in range(2):
        arrived(corner_right.at[half], c_recv.at[0, half])
        arrived(corner_left.at[half], c_recv.at[1, half])
    windows = []
    for m in range(members):
        own = whole(late.at[edge], m)
        beyond = whole(corner, m)
        side = whole(left.at[edge], m) * mc + whole(right.at[edge], m) * nc
        far = whole(corner_left, m) * mc + whole(corner_right, m) * nc
        group = []
        for middle, flank in (
            (beyond * mr + own * nr, far * mr + side * nr),
            (own * mr + beyond * nr, side * mr + far * nr),
        ):
            group.append(flank * mc + middle * nc)
            group.append(middle * mc + flank * nc)
        windows.append(group)
    finish(edge, windows, edge_bias)

    for b in range(2):
        spots = []
        for r in range(WIN):
            place = lax.rem(r + split0, WIN)
            low = jnp.where(place < split0, 1, 0)
            tile_of = low if b == 0 else 1 - low
            spots.append((tile_of, place // (WIN // 2), lax.rem(place, WIN // 2)))
        for m in range(members):
            tile = jnp.concatenate(
                [stream[t, h, m, p].reshape(1, WIN, channels) for t, h, p in spots], axis=0
            )
            tile = pltpu.roll(tile, off1, 1)
            out[m, b * WIN : (b + 1) * WIN] = tile.astype(BF)

    for copy in list(sends.values()) + backs + halo:
        copy.wait_send()


def per_device(sizes, fields, land_mask, offsets, land_embed, *weights):
    members, height, breadth, channels = fields.shape
    tokens = WIN * WIN
    part = tokens // 2
    vmem = pl.BlockSpec(memory_space=pltpu.VMEM)
    hbm = pl.BlockSpec(memory_space=pltpu.HBM)
    piece = (members, part, channels)
    dma = pltpu.SemaphoreType.DMA
    scratch = [pltpu.VMEM(w.shape, w.dtype) for w in (fields,) + weights] + [
        pltpu.VMEM((2, 2, members, WIN // 2, WIN, channels), F32),
        pltpu.VMEM((2, 2) + piece, BF),
        pltpu.VMEM((3, 2) + piece, BF),
        pltpu.VMEM((4, members, part, 3 * channels), F32),
        pltpu.VMEM((2,) + piece, F32),
        pltpu.VMEM((2,) + piece, BF),
        pltpu.VMEM((2,) + piece, BF),
        pltpu.VMEM((2, 2) + piece, BF),
        pltpu.VMEM((2, 2) + piece, BF),
        pltpu.VMEM((2, 2) + piece, BF),
        pltpu.VMEM((2, 2) + piece, BF),
        pltpu.VMEM((2,) + piece, BF),
        pltpu.VMEM((2,) + piece, BF),
        pltpu.VMEM((2,) + piece, BF),
        dma((len(weights) + 1,)),
        dma((3, 2, members)), dma((3, 2, members)), dma((2,)), dma((2,)),
        dma((2, 2)), dma((2, 2)),
        dma((2, 2)), dma((2, 2)),
        dma((2, 2)), dma((2, 2)),
        dma((2, 2)), dma((2, 2)),
    ]
    return pl.pallas_call(
        functools.partial(kernel, sizes),
        out_shape=pltpu.VMEM(fields.shape, BF),
        in_specs=[hbm, vmem, pl.BlockSpec(memory_space=pltpu.SMEM), vmem]
        + [hbm] * len(weights),
        out_specs=vmem,
        scratch_shapes=scratch,
        compiler_params=pltpu.CompilerParams(collective_id=0, has_side_effects=True, vmem_limit_bytes=VMEM_LIMIT),
        name="scorer",
    )(fields, land_mask.T, offsets, land_embed.reshape(1, channels), *weights)


def solution(mesh):
    sizes = tuple(mesh.shape[axis] for axis in ("member", "lat", "lon"))
    return jax.shard_map(
        functools.partial(per_device, sizes),
        mesh=mesh,
        in_specs=(P("member", "lat", "lon", None), P("lat", "lon")) + (P(),) * 12,
        out_specs=P("member", "lat", "lon", None),
        check_vma=False,
    )
```

```python
import functools

import jax
import jax.numpy as jnp
from jax import lax
from jax.experimental import pallas as pl
from jax.experimental.pallas import tpu as pltpu
from jax.sharding import PartitionSpec as P

HEADS = 4
WIN = 8
EPS = 1e-05
VMEM_LIMIT = 58 * 1024 * 1024
NEG = -1e30
MESH = pl.DeviceIdType.MESH
BF = jnp.bfloat16
F32 = jnp.float32


def normalize(stream):
    average = jnp.mean(stream, axis=-1, keepdims=True)
    centered = stream - average
    spread = jnp.mean(centered * centered, axis=-1, keepdims=True)
    return (centered * lax.rsqrt(spread + EPS)).astype(BF)


def project(inputs, matrix):
    return jnp.dot(inputs, matrix, preferred_element_type=F32)


def gelu(x):
    return (0.5 * x) * (1.0 + lax.erf(x * 0.7071067811865476))


def feed_forward(stream, w_up, w_down):
    hidden = gelu(project(normalize(stream), w_up)).astype(BF)
    return stream + project(hidden, w_down)


def head_masks(channels, dtype):
    lane = lax.broadcasted_iota(jnp.int32, (1, channels), 1) // (channels // HEADS)
    return [jnp.where(lane == h, 1.0, 0.0).astype(dtype) for h in range(HEADS)]


def attend(q, k, v, bias, masks_bf, masks_f32):
    count = q.shape[0]
    stacked = jnp.concatenate([q * mask for mask in masks_bf], axis=0)
    scores = lax.dot_general(
        stacked, k, (((1,), (1,)), ((), ())), preferred_element_type=F32
    )
    if bias is not None:
        scores = (
            scores.reshape(HEADS, count, -1) + bias[None]
        ).reshape(scores.shape)
    top = jnp.max(scores, axis=-1, keepdims=True)
    weights = jnp.exp(scores - top)
    total = jnp.sum(weights, axis=-1, keepdims=True)
    weights = (weights * (1.0 / total)).astype(BF)
    wide = project(weights, v)
    result = wide[:count] * masks_f32[0]
    for h in range(1, HEADS):
        result = result + wide[h * count : (h + 1) * count] * masks_f32[h]
    return result


def kernel(
    sizes,
    h_fields, land, offsets, embed,
    h_win_qkv, h_win_out, h_win_up, h_win_down, h_mem_qkv, h_mem_out,
    h_shift_qkv, h_shift_out, h_shift_up, h_shift_down,
    out,
    fields, win_qkv, win_out, win_up, win_down, mem_qkv, mem_out,
    shift_qkv, shift_out, shift_up, shift_down,
    stream, mine, got, qkv, mixed, mixed_send, mixed_got,
    late, vert, left, right, corner, corner_left, corner_right, final,
    w_sem, a_send, a_recv, r_send, r_recv, v_send, v_recv,
    l_send, l_recv, rt_send, rt_recv, c_send, c_recv,
):
    n_member, n_lat, n_lon = sizes
    members = h_fields.shape[0]
    channels = h_fields.shape[-1]
    tokens = WIN * WIN
    part = tokens // 2
    edge, inner = 0, 1
    me = lax.axis_index("member")
    lat = lax.axis_index("lat")
    lon = lax.axis_index("lon")
    core = lax.rem(me, 2)
    chip = me // 2
    other = 1 - core
    mate = {"member": 2 * chip + other}
    far_same = {"member": 2 * (1 - chip) + core}
    far_other = {"member": 2 * (1 - chip) + other}
    lat_up = {"lat": lax.rem(lat + n_lat - 1, n_lat)}
    lat_down = {"lat": lax.rem(lat + 1, n_lat)}
    lon_left = {"lon": lax.rem(lon + n_lon - 1, n_lon)}
    lon_right = {"lon": lax.rem(lon + 1, n_lon)}

    barrier = pltpu.get_barrier_semaphore()
    for peer in (mate, far_same, far_other, lat_up, lat_down, lon_left, lon_right):
        pl.semaphore_signal(barrier, inc=1, device_id=peer, device_id_type=MESH)

    pairs = [
        (h_fields, fields),
        (h_win_qkv, win_qkv), (h_win_out, win_out), (h_win_up, win_up),
        (h_win_down, win_down), (h_mem_qkv, mem_qkv), (h_mem_out, mem_out),
        (h_shift_qkv, shift_qkv), (h_shift_out, shift_out),
        (h_shift_up, shift_up), (h_shift_down, shift_down),
    ]
    loads = [
        pltpu.make_async_copy(source, target, w_sem.at[i])
        for i, (source, target) in enumerate(pairs)
    ]
    for load in loads:
        load.start()

    off0 = offsets[0]
    off1 = offsets[1]
    split0 = WIN - off0
    split1 = WIN - off1
    masks_bf = head_masks(channels, BF)
    masks_f32 = head_masks(channels, F32)
    scale = (channels // HEADS) ** -0.5

    def push(source, target, send, recv, peer):
        copy = pltpu.make_async_remote_copy(
            src_ref=source, dst_ref=target, send_sem=send, recv_sem=recv,
            device_id=peer, device_id_type=MESH,
        )
        copy.start()
        return copy

    token = lax.broadcasted_iota(jnp.int32, (tokens, channels), 0)
    is_low = token // WIN < split0
    row_low = jnp.where(is_low, 1.0, 0.0)
    col_low = jnp.where(lax.rem(token, WIN) < split1, 1.0, 0.0)

    flags = pltpu.roll(land[...].astype(F32), split1, 0)
    spread = jnp.concatenate([flags] * WIN, axis=0)
    s_row = lax.broadcasted_iota(jnp.int32, spread.shape, 0) // WIN
    s_lane = lax.broadcasted_iota(jnp.int32, spread.shape, 1)
    s_pick = lax.rem(s_row + off0, WIN)
    loads[0].wait()

    def window_section(block, waits):
        rows = [WIN * block + lax.rem(s + off0, WIN) for s in range(WIN)]
        picked = jnp.where(s_lane == WIN * block + s_pick, spread, 0.0)
        added = jnp.sum(picked, axis=-1, keepdims=True) * embed[...]
        tiles = []
        for m in range(members):
            tile = jnp.concatenate(
                [fields[m, r].astype(F32).reshape(1, WIN, channels) for r in rows], axis=0
            )
            tiles.append(pltpu.roll(tile, split1, 1).reshape(tokens, channels) + added)
        x = jnp.concatenate(tiles, axis=0)
        if waits:
            loads[1].wait()
        proj = project(normalize(x), win_qkv[...])
        atts = []
        for m in range(members):
            span = slice(m * tokens, (m + 1) * tokens)
            q = (proj[span, :channels] * scale).astype(BF)
            k = proj[span, channels : 2 * channels].astype(BF)
            v = proj[span, 2 * channels :].astype(BF)
            atts.append(attend(q, k, v, None, masks_bf, masks_f32))
        if waits:
            loads[2].wait()
        x = x + project(jnp.concatenate(atts, axis=0).astype(BF), win_out[...])
        if waits:
            loads[3].wait()
            loads[4].wait()
        x = feed_forward(x, win_up[...], win_down[...])
        normed = normalize(x)
        for m in range(members):
            for half in range(2):
                first = m * tokens + half * part
                span = slice(first, first + part)
                stream[block, half, m] = x[span].reshape(WIN // 2, WIN, channels)
                mine[block, half, m] = normed[span]

    sends = {}

    def send_members(block, i, peer):
        for half in range(2):
            sends[i, half] = push(
                mine.at[block, half], got.at[i, half], a_send.at[i, half],
                a_recv.at[i, half], peer,
            )

    window_section(other, True)
    pl.semaphore_wait(barrier, 7)
    send_members(other, 1, far_other)
    send_members(other, 0, mate)
    window_section(core, False)
    send_members(core, 2, far_same)
    loads[5].wait()
    loads[6].wait()

    near = 2 * members
    total = 4 * members
    qt = lax.rem(lax.broadcasted_iota(jnp.int32, (near * WIN, total * WIN), 0), WIN)
    kt = lax.rem(lax.broadcasted_iota(jnp.int32, (near * WIN, total * WIN), 1), WIN)
    same_token = jnp.where(qt == kt, 0.0, NEG)
    backs = []

    def member_qkv(source, x, with_q):
        weights = mem_qkv[...] if with_q else mem_qkv[:, channels:]
        first_col = 0 if with_q else channels
        qkv[source, :, :, first_col:] = project(
            x.reshape(members * part, channels), weights
        ).reshape(members, part, -1)

    def member_attention(e):
        member_qkv(0, mine[core, e], True)
        sends[0, e].wait_recv()
        member_qkv(1, got[0, e], True)
        for i in (1, 2):
            sends[i, e].wait_recv()
            member_qkv(i + 1, got[i, e], False)
        for group in range(part // WIN):
            span = slice(group * WIN, (group + 1) * WIN)
            q = qkv[0:2, :, span, 0:channels].reshape(near * WIN, channels)
            k = qkv[:, :, span, channels : 2 * channels].reshape(total * WIN, channels)
            v = qkv[:, :, span, 2 * channels :].reshape(total * WIN, channels)
            att = attend(
                (q * scale).astype(BF), k.astype(BF), v.astype(BF), same_token,
                masks_bf, masks_f32,
            )
            mixed[:, :, span, :] = att.reshape(2, members, WIN, channels)
        mixed_send[e] = mixed[1].astype(BF)
        backs.append(
            push(mixed_send.at[e], mixed_got.at[e], r_send.at[e], r_recv.at[e], mate)
        )

    def member_add(e, half, att):
        x = stream[e, half].reshape(members * part, channels)
        x = x + project(att.reshape(members * part, channels), mem_out[...])
        stream[e, half] = x.reshape(members, WIN // 2, WIN, channels)
        late[e, half] = normalize(x).reshape(members, part, channels)

    halo = []

    def send_halo(block, half):
        piece = late.at[block, half]
        toward = {"lat": lax.rem(lat + 2 * block - 1 + n_lat, n_lat)}
        for target, send, recv, peer in (
            (vert.at[1 - block, half], v_send.at[block, half], v_recv.at[1 - block, half], toward),
            (right.at[block, half], l_send.at[block, half], l_recv.at[block, half], lon_left),
            (left.at[block, half], rt_send.at[block, half], rt_recv.at[block, half], lon_right),
        ):
            halo.append(push(piece, target, send, recv, peer))

    def arrived(buffer, sem):
        pltpu.make_async_copy(buffer, buffer, sem).wait()

    for half in range(2):
        member_attention(half)
        member_add(core, half, mixed[0].astype(BF))
        send_halo(core, half)
    for half in range(2):
        arrived(mixed_got.at[half], r_recv.at[half])
        member_add(other, half, mixed_got[half])
        send_halo(other, half)

    mr, nr = row_low.astype(BF), (1.0 - row_low).astype(BF)
    mc, nc = col_low.astype(BF), (1.0 - col_low).astype(BF)

    def relay(half):
        arrived(vert.at[0, half], v_recv.at[0, half])
        arrived(vert.at[1, half], v_recv.at[1, half])
        h_tok = lax.broadcasted_iota(jnp.int32, (part, channels), 0) + half * part
        h_low = jnp.where(h_tok // WIN < split0, 1.0, 0.0)
        h_mr, h_nr = h_low.astype(BF), (1.0 - h_low).astype(BF)
        corner[half] = vert[0, half] * h_mr[None] + vert[1, half] * h_nr[None]
        halo.append(
            push(corner.at[half], corner_right.at[half], c_send.at[0, half],
                 c_recv.at[0, half], lon_left)
        )
        halo.append(
            push(corner.at[half], corner_left.at[half], c_send.at[1, half],
                 c_recv.at[1, half], lon_right)
        )

    relay(0)
    relay(1)

    q_tok = lax.broadcasted_iota(jnp.int32, (tokens, 4 * tokens), 0)
    k_tok = lax.broadcasted_iota(jnp.int32, (tokens, 4 * tokens), 1)
    q_row = jnp.where(q_tok // WIN < split0, 1, 0)
    q_col = jnp.where(lax.rem(q_tok, WIN) < split1, 1, 0)
    k_row = k_tok // (2 * tokens)
    k_col = lax.rem(k_tok // tokens, 2)
    k_low = jnp.where(lax.rem(k_tok, tokens) // WIN < split0, 1, 0)
    col_bias = jnp.where(q_col == k_col, 0.0, NEG)
    first = jnp.where(lat == 0, 1.0, 0.0)
    last = jnp.where(lat == n_lat - 1, 1.0, 0.0)
    outside = jnp.where(k_row == 0, jnp.where(k_low == 1, NEG, 0.0), 0.0) * first
    outside = outside + jnp.where(k_row == 1, jnp.where(k_low == 0, NEG, 0.0), 0.0) * last
    edge_bias = jnp.where(q_row == k_row, 0.0, NEG) + col_bias + outside
    inner_bias = col_bias[:, : 2 * tokens]

    for load in loads[7:]:
        load.wait()

    def whole(ref, m):
        return ref[:, m].reshape(tokens, channels)

    def joined(ref, e, m):
        return whole(ref.at[1 - e], m) * mr + whole(ref.at[e], m) * nr

    def finish(e, windows, bias):
        count = len(windows[0]) * tokens
        own = jnp.concatenate([joined(late, e, m) for m in range(members)], axis=0)
        asked = (project(own, shift_qkv[:, :channels]) * scale).astype(BF)
        keyed = project(
            jnp.concatenate([w for group in windows for w in group], axis=0),
            shift_qkv[:, channels:],
        ).astype(BF)
        atts = []
        for m in range(members):
            keys = slice(m * count, (m + 1) * count)
            atts.append(
                attend(
                    asked[m * tokens : (m + 1) * tokens], keyed[keys, :channels],
                    keyed[keys, channels:], bias, masks_bf, masks_f32,
                )
            )
        x = jnp.concatenate(
            [
                jnp.where(
                    is_low,
                    stream[1 - e, :, m].reshape(tokens, channels),
                    stream[e, :, m].reshape(tokens, channels),
                )
                for m in range(members)
            ],
            axis=0,
        )
        x = x + project(jnp.concatenate(atts, axis=0).astype(BF), shift_out[...])
        x = feed_forward(x, shift_up[...], shift_down[...])
        for m in range(members):
            final[e, :, m] = x[m * tokens : (m + 1) * tokens].reshape(
                2, WIN // 2, WIN, channels
            )

    for block in range(2):
        for half in range(2):
            arrived(right.at[block, half], l_recv.at[block, half])
            arrived(left.at[block, half], rt_recv.at[block, half])
    windows = []
    for m in range(members):
        own = joined(late, inner, m)
        windows.append(
            [
                joined(left, inner, m) * mc + own * nc,
                own * mc + joined(right, inner, m) * nc,
            ]
        )
    finish(inner, windows, inner_bias)

    for half in range(2):
        arrived(corner_right.at[half], c_recv.at[0, half])
        arrived(corner_left.at[half], c_recv.at[1, half])
    windows = []
    for m in range(members):
        own = joined(late, edge, m)
        beyond = whole(corner, m)
        side = joined(left, edge, m) * mc + joined(right, edge, m) * nc
        far = whole(corner_left, m) * mc + whole(corner_right, m) * nc
        group = []
        for middle, flank in (
            (beyond * mr + own * nr, far * mr + side * nr),
            (own * mr + beyond * nr, side * mr + far * nr),
        ):
            group.append(flank * mc + middle * nc)
            group.append(middle * mc + flank * nc)
        windows.append(group)
    finish(edge, windows, edge_bias)

    for b in range(2):
        spots = []
        for r in range(WIN):
            place = lax.rem(r + split0, WIN)
            low = jnp.where(place < split0, 1, 0)
            tile_of = low if b == 0 else 1 - low
            spots.append((tile_of, place // (WIN // 2), lax.rem(place, WIN // 2)))
        for m in range(members):
            tile = jnp.concatenate(
                [final[t, h, m, p].reshape(1, WIN, channels) for t, h, p in spots], axis=0
            )
            tile = pltpu.roll(tile, off1, 1)
            out[m, b * WIN : (b + 1) * WIN] = tile.astype(BF)

    for copy in list(sends.values()) + backs + halo:
        copy.wait_send()


def per_device(sizes, fields, land_mask, offsets, land_embed, *weights):
    members, height, breadth, channels = fields.shape
    tokens = WIN * WIN
    part = tokens // 2
    vmem = pl.BlockSpec(memory_space=pltpu.VMEM)
    hbm = pl.BlockSpec(memory_space=pltpu.HBM)
    piece = (members, part, channels)
    dma = pltpu.SemaphoreType.DMA
    scratch = [pltpu.VMEM(w.shape, w.dtype) for w in (fields,) + weights] + [
        pltpu.VMEM((2, 2, members, WIN // 2, WIN, channels), F32),
        pltpu.VMEM((2, 2) + piece, BF),
        pltpu.VMEM((3, 2) + piece, BF),
        pltpu.VMEM((4, members, part, 3 * channels), F32),
        pltpu.VMEM((2,) + piece, F32),
        pltpu.VMEM((2,) + piece, BF),
        pltpu.VMEM((2,) + piece, BF),
        pltpu.VMEM((2, 2) + piece, BF),
        pltpu.VMEM((2, 2) + piece, BF),
        pltpu.VMEM((2, 2) + piece, BF),
        pltpu.VMEM((2, 2) + piece, BF),
        pltpu.VMEM((2,) + piece, BF),
        pltpu.VMEM((2,) + piece, BF),
        pltpu.VMEM((2,) + piece, BF),
        pltpu.VMEM((2, 2, members, WIN // 2, WIN, channels), F32),
        dma((len(weights) + 1,)),
        dma((3, 2)), dma((3, 2)), dma((2,)), dma((2,)),
        dma((2, 2)), dma((2, 2)),
        dma((2, 2)), dma((2, 2)),
        dma((2, 2)), dma((2, 2)),
        dma((2, 2)), dma((2, 2)),
    ]
    return pl.pallas_call(
        functools.partial(kernel, sizes),
        out_shape=pltpu.VMEM(fields.shape, BF),
        in_specs=[hbm, vmem, pl.BlockSpec(memory_space=pltpu.SMEM), vmem]
        + [hbm] * len(weights),
        out_specs=vmem,
        scratch_shapes=scratch,
        compiler_params=pltpu.CompilerParams(collective_id=0, has_side_effects=True, vmem_limit_bytes=VMEM_LIMIT),
        name="scorer",
    )(fields, land_mask.T, offsets, land_embed.reshape(1, channels), *weights)


def solution(mesh):
    sizes = tuple(mesh.shape[axis] for axis in ("member", "lat", "lon"))
    return jax.shard_map(
        functools.partial(per_device, sizes),
        mesh=mesh,
        in_specs=(P("member", "lat", "lon", None), P("lat", "lon")) + (P(),) * 12,
        out_specs=P("member", "lat", "lon", None),
        check_vma=False,
    )
```

```python
import functools

import jax
import jax.numpy as jnp
from jax import lax
from jax.experimental import pallas as pl
from jax.experimental.pallas import tpu as pltpu
from jax.sharding import PartitionSpec as P

HEADS = 4
WIN = 8
EPS = 1e-05
VMEM_LIMIT = 58 * 1024 * 1024
NEG = -1e30
MESH = pl.DeviceIdType.MESH
BF = jnp.bfloat16
F32 = jnp.float32


def normalize(stream):
    average = jnp.mean(stream, axis=-1, keepdims=True)
    centered = stream - average
    spread = jnp.mean(centered * centered, axis=-1, keepdims=True)
    return (centered * lax.rsqrt(spread + EPS)).astype(BF)


def project(inputs, matrix):
    return jnp.dot(inputs, matrix, preferred_element_type=F32)


def gelu(x):
    return (0.5 * x) * (1.0 + lax.erf(x * 0.7071067811865476))


def feed_forward(stream, w_up, w_down):
    hidden = gelu(project(normalize(stream), w_up)).astype(BF)
    return stream + project(hidden, w_down)


def head_masks(channels, dtype):
    lane = lax.broadcasted_iota(jnp.int32, (1, channels), 1) // (channels // HEADS)
    return [jnp.where(lane == h, 1.0, 0.0).astype(dtype) for h in range(HEADS)]


def attend(q, k, v, bias, masks_bf, masks_f32):
    count = q.shape[0]
    stacked = jnp.concatenate([q * mask for mask in masks_bf], axis=0)
    scores = lax.dot_general(
        stacked, k, (((1,), (1,)), ((), ())), preferred_element_type=F32
    )
    if bias is not None:
        scores = (
            scores.reshape(HEADS, count, -1) + bias[None]
        ).reshape(scores.shape)
    top = jnp.max(scores, axis=-1, keepdims=True)
    weights = jnp.exp(scores - top)
    total = jnp.sum(weights, axis=-1, keepdims=True)
    weights = (weights * (1.0 / total)).astype(BF)
    wide = project(weights, v)
    result = wide[:count] * masks_f32[0]
    for h in range(1, HEADS):
        result = result + wide[h * count : (h + 1) * count] * masks_f32[h]
    return result


def kernel(
    sizes,
    h_fields, land, offsets, embed,
    h_win_qkv, h_win_out, h_win_up, h_win_down, h_mem_qkv, h_mem_out,
    h_shift_qkv, h_shift_out, h_shift_up, h_shift_down,
    out,
    fields, win_qkv, win_out, win_up, win_down, mem_qkv, mem_out,
    shift_qkv, shift_out, shift_up, shift_down,
    stream, mine, got, qkv, mixed, mixed_send, mixed_got,
    late, vert, left, right, corner, corner_left, corner_right, final,
    w_sem, a_send, a_recv, r_send, r_recv, v_send, v_recv,
    l_send, l_recv, rt_send, rt_recv, c_send, c_recv,
):
    n_member, n_lat, n_lon = sizes
    members = h_fields.shape[0]
    channels = h_fields.shape[-1]
    tokens = WIN * WIN
    part = tokens // 2
    edge, inner = 0, 1
    me = lax.axis_index("member")
    lat = lax.axis_index("lat")
    lon = lax.axis_index("lon")
    core = lax.rem(me, 2)
    chip = me // 2
    other = 1 - core
    mate = {"member": 2 * chip + other}
    far_same = {"member": 2 * (1 - chip) + core}
    far_other = {"member": 2 * (1 - chip) + other}
    lat_up = {"lat": lax.rem(lat + n_lat - 1, n_lat)}
    lat_down = {"lat": lax.rem(lat + 1, n_lat)}
    lon_left = {"lon": lax.rem(lon + n_lon - 1, n_lon)}
    lon_right = {"lon": lax.rem(lon + 1, n_lon)}

    barrier = pltpu.get_barrier_semaphore()
    for peer in (mate, far_same, far_other, lat_up, lat_down, lon_left, lon_right):
        pl.semaphore_signal(barrier, inc=1, device_id=peer, device_id_type=MESH)

    pairs = [
        (h_fields, fields),
        (h_win_qkv, win_qkv), (h_win_out, win_out), (h_win_up, win_up),
        (h_win_down, win_down), (h_mem_qkv, mem_qkv), (h_mem_out, mem_out),
        (h_shift_qkv, shift_qkv), (h_shift_out, shift_out),
        (h_shift_up, shift_up), (h_shift_down, shift_down),
    ]
    loads = [
        pltpu.make_async_copy(source, target, w_sem.at[i])
        for i, (source, target) in enumerate(pairs)
    ]
    for load in loads:
        load.start()

    off0 = offsets[0]
    off1 = offsets[1]
    split0 = WIN - off0
    split1 = WIN - off1
    masks_bf = head_masks(channels, BF)
    masks_f32 = head_masks(channels, F32)
    scale = (channels // HEADS) ** -0.5

    def push(source, target, send, recv, peer):
        copy = pltpu.make_async_remote_copy(
            src_ref=source, dst_ref=target, send_sem=send, recv_sem=recv,
            device_id=peer, device_id_type=MESH,
        )
        copy.start()
        return copy

    token = lax.broadcasted_iota(jnp.int32, (tokens, channels), 0)
    is_low = token // WIN < split0
    row_low = jnp.where(is_low, 1.0, 0.0)
    col_low = jnp.where(lax.rem(token, WIN) < split1, 1.0, 0.0)

    flags = pltpu.roll(land[...].astype(F32), split1, 0)
    spread = jnp.concatenate([flags] * WIN, axis=0)
    s_row = lax.broadcasted_iota(jnp.int32, spread.shape, 0) // WIN
    s_lane = lax.broadcasted_iota(jnp.int32, spread.shape, 1)
    s_pick = lax.rem(s_row + off0, WIN)
    loads[0].wait()

    def window_section(block, waits):
        rows = [WIN * block + lax.rem(s + off0, WIN) for s in range(WIN)]
        picked = jnp.where(s_lane == WIN * block + s_pick, spread, 0.0)
        added = jnp.sum(picked, axis=-1, keepdims=True) * embed[...]
        tiles = []
        for m in range(members):
            tile = jnp.concatenate(
                [fields[m, r].astype(F32).reshape(1, WIN, channels) for r in rows], axis=0
            )
            tiles.append(pltpu.roll(tile, split1, 1).reshape(tokens, channels) + added)
        x = jnp.concatenate(tiles, axis=0)
        if waits:
            loads[1].wait()
        proj = project(normalize(x), win_qkv[...])
        atts = []
        for m in range(members):
            span = slice(m * tokens, (m + 1) * tokens)
            q = (proj[span, :channels] * scale).astype(BF)
            k = proj[span, channels : 2 * channels].astype(BF)
            v = proj[span, 2 * channels :].astype(BF)
            atts.append(attend(q, k, v, None, masks_bf, masks_f32))
        if waits:
            loads[2].wait()
        x = x + project(jnp.concatenate(atts, axis=0).astype(BF), win_out[...])
        if waits:
            loads[3].wait()
            loads[4].wait()
        x = feed_forward(x, win_up[...], win_down[...])
        normed = normalize(x)
        for m in range(members):
            for half in range(2):
                first = m * tokens + half * part
                span = slice(first, first + part)
                stream[block, half, m] = x[span].reshape(WIN // 2, WIN, channels)
                mine[block, half, m] = normed[span]

    sends = {}

    def send_members(block):
        for i, (half, peer) in enumerate(
            ((other, mate), (other, far_other), (core, far_same))
        ):
            sends[i, block] = push(
                mine.at[block, half], got.at[i, block], a_send.at[i, block],
                a_recv.at[i, block], peer,
            )

    window_section(0, True)
    pl.semaphore_wait(barrier, 7)
    send_members(0)
    window_section(1, False)
    send_members(1)
    loads[5].wait()
    loads[6].wait()

    near = 2 * members
    total = 4 * members
    qt = lax.rem(lax.broadcasted_iota(jnp.int32, (near * WIN, total * WIN), 0), WIN)
    kt = lax.rem(lax.broadcasted_iota(jnp.int32, (near * WIN, total * WIN), 1), WIN)
    same_token = jnp.where(qt == kt, 0.0, NEG)
    backs = []

    def member_qkv(source, x, with_q):
        weights = mem_qkv[...] if with_q else mem_qkv[:, channels:]
        first_col = 0 if with_q else channels
        qkv[source, :, :, first_col:] = project(
            x.reshape(members * part, channels), weights
        ).reshape(members, part, -1)

    def member_attention(e):
        member_qkv(0, mine[e, core], True)
        sends[0, e].wait_recv()
        member_qkv(1, got[0, e], True)
        for i in (1, 2):
            sends[i, e].wait_recv()
            member_qkv(i + 1, got[i, e], False)
        for group in range(part // WIN):
            span = slice(group * WIN, (group + 1) * WIN)
            q = qkv[0:2, :, span, 0:channels].reshape(near * WIN, channels)
            k = qkv[:, :, span, channels : 2 * channels].reshape(total * WIN, channels)
            v = qkv[:, :, span, 2 * channels :].reshape(total * WIN, channels)
            att = attend(
                (q * scale).astype(BF), k.astype(BF), v.astype(BF), same_token,
                masks_bf, masks_f32,
            )
            mixed[:, :, span, :] = att.reshape(2, members, WIN, channels)
        mixed_send[e] = mixed[1].astype(BF)
        backs.append(
            push(mixed_send.at[e], mixed_got.at[e], r_send.at[e], r_recv.at[e], mate)
        )

    def member_add(e, half, att):
        x = stream[e, half].reshape(members * part, channels)
        x = x + project(att.reshape(members * part, channels), mem_out[...])
        stream[e, half] = x.reshape(members, WIN // 2, WIN, channels)
        late[e, half] = normalize(x).reshape(members, part, channels)

    halo = []

    def send_halo(block, half):
        piece = late.at[block, half]
        toward = {"lat": lax.rem(lat + 2 * block - 1 + n_lat, n_lat)}
        for target, send, recv, peer in (
            (vert.at[1 - block, half], v_send.at[block, half], v_recv.at[1 - block, half], toward),
            (right.at[block, half], l_send.at[block, half], l_recv.at[block, half], lon_left),
            (left.at[block, half], rt_send.at[block, half], rt_recv.at[block, half], lon_right),
        ):
            halo.append(push(piece, target, send, recv, peer))

    def arrived(buffer, sem):
        pltpu.make_async_copy(buffer, buffer, sem).wait()

    for block in range(2):
        member_attention(block)
        member_add(block, core, mixed[0].astype(BF))
        send_halo(block, core)
        arrived(mixed_got.at[block], r_recv.at[block])
        member_add(block, other, mixed_got[block])
        send_halo(block, other)

    mr, nr = row_low.astype(BF), (1.0 - row_low).astype(BF)
    mc, nc = col_low.astype(BF), (1.0 - col_low).astype(BF)

    def relay(half):
        arrived(vert.at[0, half], v_recv.at[0, half])
        arrived(vert.at[1, half], v_recv.at[1, half])
        h_tok = lax.broadcasted_iota(jnp.int32, (part, channels), 0) + half * part
        h_low = jnp.where(h_tok // WIN < split0, 1.0, 0.0)
        h_mr, h_nr = h_low.astype(BF), (1.0 - h_low).astype(BF)
        corner[half] = vert[0, half] * h_mr[None] + vert[1, half] * h_nr[None]
        halo.append(
            push(corner.at[half], corner_right.at[half], c_send.at[0, half],
                 c_recv.at[0, half], lon_left)
        )
        halo.append(
            push(corner.at[half], corner_left.at[half], c_send.at[1, half],
                 c_recv.at[1, half], lon_right)
        )

    relay(core)
    relay(other)

    q_tok = lax.broadcasted_iota(jnp.int32, (tokens, 4 * tokens), 0)
    k_tok = lax.broadcasted_iota(jnp.int32, (tokens, 4 * tokens), 1)
    q_row = jnp.where(q_tok // WIN < split0, 1, 0)
    q_col = jnp.where(lax.rem(q_tok, WIN) < split1, 1, 0)
    k_row = k_tok // (2 * tokens)
    k_col = lax.rem(k_tok // tokens, 2)
    k_low = jnp.where(lax.rem(k_tok, tokens) // WIN < split0, 1, 0)
    col_bias = jnp.where(q_col == k_col, 0.0, NEG)
    first = jnp.where(lat == 0, 1.0, 0.0)
    last = jnp.where(lat == n_lat - 1, 1.0, 0.0)
    outside = jnp.where(k_row == 0, jnp.where(k_low == 1, NEG, 0.0), 0.0) * first
    outside = outside + jnp.where(k_row == 1, jnp.where(k_low == 0, NEG, 0.0), 0.0) * last
    edge_bias = jnp.where(q_row == k_row, 0.0, NEG) + col_bias + outside
    inner_bias = col_bias[:, : 2 * tokens]

    for load in loads[7:]:
        load.wait()

    def whole(ref, m):
        return ref[:, m].reshape(tokens, channels)

    def joined(ref, e, m):
        return whole(ref.at[1 - e], m) * mr + whole(ref.at[e], m) * nr

    def stacked(pieces):
        return jnp.concatenate(pieces, axis=0)

    def ask(owns):
        return (project(stacked(owns), shift_qkv[:, :channels]) * scale).astype(BF)

    def to_keyed(pieces):
        return project(stacked(pieces), shift_qkv[:, channels:]).astype(BF)

    def residual(e):
        return stacked(
            [
                jnp.where(
                    is_low,
                    stream[1 - e, :, m].reshape(tokens, channels),
                    stream[e, :, m].reshape(tokens, channels),
                )
                for m in range(members)
            ]
        )

    def finish(e, x, asked, keyed, bias):
        atts = []
        for m in range(members):
            atts.append(
                attend(
                    asked[m * tokens : (m + 1) * tokens], keyed[m][:, :channels],
                    keyed[m][:, channels:], bias, masks_bf, masks_f32,
                )
            )
        x = x + project(stacked(atts).astype(BF), shift_out[...])
        x = feed_forward(x, shift_up[...], shift_down[...])
        for m in range(members):
            final[e, :, m] = x[m * tokens : (m + 1) * tokens].reshape(
                2, WIN // 2, WIN, channels
            )

    for block in range(2):
        for half in range(2):
            arrived(right.at[block, half], l_recv.at[block, half])
            arrived(left.at[block, half], rt_recv.at[block, half])
    owns = [joined(late, inner, m) for m in range(members)]
    windows = []
    for m in range(members):
        windows.append(joined(left, inner, m) * mc + owns[m] * nc)
        windows.append(owns[m] * mc + joined(right, inner, m) * nc)
    keyed = to_keyed(windows)
    keyed = [keyed[2 * m * tokens : 2 * (m + 1) * tokens] for m in range(members)]
    finish(inner, residual(inner), ask(owns), keyed, inner_bias)

    owns = [joined(late, edge, m) for m in range(members)]
    sides = [
        joined(left, edge, m) * mc + joined(right, edge, m) * nc for m in range(members)
    ]
    beyonds = [whole(corner, m) for m in range(members)]
    known = to_keyed(owns + sides + beyonds)
    edge_asked = ask(owns)
    edge_x = residual(edge)
    mr2, nr2 = [jnp.concatenate([mask, mask], axis=1) for mask in (mr, nr)]
    mc2, nc2 = [jnp.concatenate([mask, mask], axis=1) for mask in (mc, nc)]

    def piece_of(array, index):
        return array[index * tokens : (index + 1) * tokens]

    middles = []
    for m in range(members):
        own, beyond = piece_of(known, m), piece_of(known, 2 * members + m)
        middles.append((beyond * mr2 + own * nr2, own * mr2 + beyond * nr2))
    for half in range(2):
        arrived(corner_right.at[half], c_recv.at[0, half])
        arrived(corner_left.at[half], c_recv.at[1, half])
    fars = to_keyed(
        [whole(corner_left, m) * mc + whole(corner_right, m) * nc for m in range(members)]
    )
    keyed = []
    for m in range(members):
        side, far = piece_of(known, members + m), piece_of(fars, m)
        group = []
        for middle, flank in zip(
            middles[m], (far * mr2 + side * nr2, side * mr2 + far * nr2)
        ):
            group.append(flank * mc2 + middle * nc2)
            group.append(middle * mc2 + flank * nc2)
        keyed.append(stacked(group))
    finish(edge, edge_x, edge_asked, keyed, edge_bias)

    for b in range(2):
        spots = []
        for r in range(WIN):
            place = lax.rem(r + split0, WIN)
            low = jnp.where(place < split0, 1, 0)
            tile_of = low if b == 0 else 1 - low
            spots.append((tile_of, place // (WIN // 2), lax.rem(place, WIN // 2)))
        for m in range(members):
            tile = jnp.concatenate(
                [final[t, h, m, p].reshape(1, WIN, channels) for t, h, p in spots], axis=0
            )
            tile = pltpu.roll(tile, off1, 1)
            out[m, b * WIN : (b + 1) * WIN] = tile.astype(BF)

    for copy in list(sends.values()) + backs + halo:
        copy.wait_send()


def per_device(sizes, fields, land_mask, offsets, land_embed, *weights):
    members, height, breadth, channels = fields.shape
    tokens = WIN * WIN
    part = tokens // 2
    vmem = pl.BlockSpec(memory_space=pltpu.VMEM)
    hbm = pl.BlockSpec(memory_space=pltpu.HBM)
    piece = (members, part, channels)
    dma = pltpu.SemaphoreType.DMA
    scratch = [pltpu.VMEM(w.shape, w.dtype) for w in (fields,) + weights] + [
        pltpu.VMEM((2, 2, members, WIN // 2, WIN, channels), F32),
        pltpu.VMEM((2, 2) + piece, BF),
        pltpu.VMEM((3, 2) + piece, BF),
        pltpu.VMEM((4, members, part, 3 * channels), F32),
        pltpu.VMEM((2,) + piece, F32),
        pltpu.VMEM((2,) + piece, BF),
        pltpu.VMEM((2,) + piece, BF),
        pltpu.VMEM((2, 2) + piece, BF),
        pltpu.VMEM((2, 2) + piece, BF),
        pltpu.VMEM((2, 2) + piece, BF),
        pltpu.VMEM((2, 2) + piece, BF),
        pltpu.VMEM((2,) + piece, BF),
        pltpu.VMEM((2,) + piece, BF),
        pltpu.VMEM((2,) + piece, BF),
        pltpu.VMEM((2, 2, members, WIN // 2, WIN, channels), F32),
        dma((len(weights) + 1,)),
        dma((3, 2)), dma((3, 2)), dma((2,)), dma((2,)),
        dma((2, 2)), dma((2, 2)),
        dma((2, 2)), dma((2, 2)),
        dma((2, 2)), dma((2, 2)),
        dma((2, 2)), dma((2, 2)),
    ]
    return pl.pallas_call(
        functools.partial(kernel, sizes),
        out_shape=pltpu.VMEM(fields.shape, BF),
        in_specs=[hbm, vmem, pl.BlockSpec(memory_space=pltpu.SMEM), vmem]
        + [hbm] * len(weights),
        out_specs=vmem,
        scratch_shapes=scratch,
        compiler_params=pltpu.CompilerParams(collective_id=0, has_side_effects=True, vmem_limit_bytes=VMEM_LIMIT),
        name="scorer",
    )(fields, land_mask.T, offsets, land_embed.reshape(1, channels), *weights)


def solution(mesh):
    sizes = tuple(mesh.shape[axis] for axis in ("member", "lat", "lon"))
    return jax.shard_map(
        functools.partial(per_device, sizes),
        mesh=mesh,
        in_specs=(P("member", "lat", "lon", None), P("lat", "lon")) + (P(),) * 12,
        out_specs=P("member", "lat", "lon", None),
        check_vma=False,
    )
```

```python
import functools

import jax
import jax.numpy as jnp
from jax import lax
from jax.experimental import pallas as pl
from jax.experimental.pallas import tpu as pltpu
from jax.sharding import PartitionSpec as P

HEADS = 4
WIN = 8
EPS = 1e-05
VMEM_LIMIT = 58 * 1024 * 1024
NEG = -1e30
MESH = pl.DeviceIdType.MESH
BF = jnp.bfloat16
F32 = jnp.float32


def normalize(stream):
    average = jnp.mean(stream, axis=-1, keepdims=True)
    centered = stream - average
    spread = jnp.mean(centered * centered, axis=-1, keepdims=True)
    return (centered * lax.rsqrt(spread + EPS)).astype(BF)


def project(inputs, matrix):
    return jnp.dot(inputs, matrix, preferred_element_type=F32)


def gelu(x):
    return (0.5 * x) * (1.0 + lax.erf(x * 0.7071067811865476))


def feed_forward(stream, w_up, w_down):
    hidden = gelu(project(normalize(stream), w_up)).astype(BF)
    return stream + project(hidden, w_down)


def head_masks(channels, dtype):
    lane = lax.broadcasted_iota(jnp.int32, (1, channels), 1) // (channels // HEADS)
    return [jnp.where(lane == h, 1.0, 0.0).astype(dtype) for h in range(HEADS)]


def attend(q, k, v, bias, masks_bf, masks_f32):
    count = q.shape[0]
    stacked = jnp.concatenate([q * mask for mask in masks_bf], axis=0)
    scores = lax.dot_general(
        stacked, k, (((1,), (1,)), ((), ())), preferred_element_type=F32
    )
    if bias is not None:
        scores = (
            scores.reshape(HEADS, count, -1) + bias[None]
        ).reshape(scores.shape)
    top = jnp.max(scores, axis=-1, keepdims=True)
    weights = jnp.exp(scores - top)
    total = jnp.sum(weights, axis=-1, keepdims=True)
    weights = (weights * (1.0 / total)).astype(BF)
    wide = project(weights, v)
    result = wide[:count] * masks_f32[0]
    for h in range(1, HEADS):
        result = result + wide[h * count : (h + 1) * count] * masks_f32[h]
    return result


def kernel(
    sizes,
    h_fields, land, offsets, embed,
    h_win_qkv, h_win_out, h_win_up, h_win_down, h_mem_qkv, h_mem_out,
    h_shift_qkv, h_shift_out, h_shift_up, h_shift_down,
    out,
    fields, win_qkv, win_out, win_up, win_down, mem_qkv, mem_out,
    shift_qkv, shift_out, shift_up, shift_down,
    stream, mine, got, qkv, mixed, mixed_send, mixed_got,
    late, vert, left, right, corner, corner_left, corner_right, final,
    w_sem, a_send, a_recv, r_send, r_recv, v_send, v_recv,
    l_send, l_recv, rt_send, rt_recv, c_send, c_recv,
):
    n_member, n_lat, n_lon = sizes
    members = h_fields.shape[0]
    channels = h_fields.shape[-1]
    tokens = WIN * WIN
    part = tokens // 2
    edge, inner = 0, 1
    me = lax.axis_index("member")
    lat = lax.axis_index("lat")
    lon = lax.axis_index("lon")
    core = lax.rem(me, 2)
    chip = me // 2
    other = 1 - core
    mate = {"member": 2 * chip + other}
    far_same = {"member": 2 * (1 - chip) + core}
    far_other = {"member": 2 * (1 - chip) + other}
    lat_up = {"lat": lax.rem(lat + n_lat - 1, n_lat)}
    lat_down = {"lat": lax.rem(lat + 1, n_lat)}
    lon_left = {"lon": lax.rem(lon + n_lon - 1, n_lon)}
    lon_right = {"lon": lax.rem(lon + 1, n_lon)}

    barrier = pltpu.get_barrier_semaphore()
    for peer in (mate, far_same, far_other, lat_up, lat_down, lon_left, lon_right):
        pl.semaphore_signal(barrier, inc=1, device_id=peer, device_id_type=MESH)

    pairs = [
        (h_fields, fields),
        (h_win_qkv, win_qkv), (h_win_out, win_out), (h_win_up, win_up),
        (h_win_down, win_down), (h_mem_qkv, mem_qkv), (h_mem_out, mem_out),
        (h_shift_qkv, shift_qkv), (h_shift_out, shift_out),
        (h_shift_up, shift_up), (h_shift_down, shift_down),
    ]
    loads = [
        pltpu.make_async_copy(source, target, w_sem.at[i])
        for i, (source, target) in enumerate(pairs)
    ]
    for load in loads:
        load.start()

    off0 = offsets[0]
    off1 = offsets[1]
    split0 = WIN - off0
    split1 = WIN - off1
    masks_bf = head_masks(channels, BF)
    masks_f32 = head_masks(channels, F32)
    scale = (channels // HEADS) ** -0.5

    def push(source, target, send, recv, peer):
        copy = pltpu.make_async_remote_copy(
            src_ref=source, dst_ref=target, send_sem=send, recv_sem=recv,
            device_id=peer, device_id_type=MESH,
        )
        copy.start()
        return copy

    token = lax.broadcasted_iota(jnp.int32, (tokens, channels), 0)
    is_low = token // WIN < split0
    row_low = jnp.where(is_low, 1.0, 0.0)
    col_low = jnp.where(lax.rem(token, WIN) < split1, 1.0, 0.0)

    flags = pltpu.roll(land[...].astype(F32), split1, 0)
    spread = jnp.concatenate([flags] * WIN, axis=0)
    s_row = lax.broadcasted_iota(jnp.int32, spread.shape, 0) // WIN
    s_lane = lax.broadcasted_iota(jnp.int32, spread.shape, 1)
    s_pick = lax.rem(s_row + off0, WIN)
    loads[0].wait()

    def window_section(block, waits):
        rows = [WIN * block + lax.rem(s + off0, WIN) for s in range(WIN)]
        picked = jnp.where(s_lane == WIN * block + s_pick, spread, 0.0)
        added = jnp.sum(picked, axis=-1, keepdims=True) * embed[...]
        tiles = []
        for m in range(members):
            tile = jnp.concatenate(
                [fields[m, r].astype(F32).reshape(1, WIN, channels) for r in rows], axis=0
            )
            tiles.append(pltpu.roll(tile, split1, 1).reshape(tokens, channels) + added)
        x = jnp.concatenate(tiles, axis=0)
        if waits:
            loads[1].wait()
        proj = project(normalize(x), win_qkv[...])
        atts = []
        for m in range(members):
            span = slice(m * tokens, (m + 1) * tokens)
            q = (proj[span, :channels] * scale).astype(BF)
            k = proj[span, channels : 2 * channels].astype(BF)
            v = proj[span, 2 * channels :].astype(BF)
            atts.append(attend(q, k, v, None, masks_bf, masks_f32))
        if waits:
            loads[2].wait()
        x = x + project(jnp.concatenate(atts, axis=0).astype(BF), win_out[...])
        if waits:
            loads[3].wait()
            loads[4].wait()
        x = feed_forward(x, win_up[...], win_down[...])
        normed = normalize(x)
        for m in range(members):
            for half in range(2):
                first = m * tokens + half * part
                span = slice(first, first + part)
                stream[block, half, m] = x[span].reshape(WIN // 2, WIN, channels)
                mine[block, half, m] = normed[span]

    sends = {}

    def send_members(block, i, peer):
        for half in range(2):
            sends[i, half] = push(
                mine.at[block, half], got.at[i, half], a_send.at[i, half],
                a_recv.at[i, half], peer,
            )

    window_section(other, True)
    pl.semaphore_wait(barrier, 7)
    send_members(other, 1, far_other)
    send_members(other, 0, mate)
    window_section(core, False)
    send_members(core, 2, far_same)
    loads[5].wait()
    loads[6].wait()

    near = 2 * members
    total = 4 * members
    qt = lax.rem(lax.broadcasted_iota(jnp.int32, (near * WIN, total * WIN), 0), WIN)
    kt = lax.rem(lax.broadcasted_iota(jnp.int32, (near * WIN, total * WIN), 1), WIN)
    same_token = jnp.where(qt == kt, 0.0, NEG)
    backs = []

    def member_qkv(source, x, with_q):
        weights = mem_qkv[...] if with_q else mem_qkv[:, channels:]
        first_col = 0 if with_q else channels
        qkv[source, :, :, first_col:] = project(
            x.reshape(members * part, channels), weights
        ).reshape(members, part, -1)

    def member_attention(e):
        member_qkv(0, mine[core, e], True)
        sends[0, e].wait_recv()
        member_qkv(1, got[0, e], True)
        for i in (1, 2):
            sends[i, e].wait_recv()
            member_qkv(i + 1, got[i, e], False)
        for group in range(part // WIN):
            span = slice(group * WIN, (group + 1) * WIN)
            q = qkv[0:2, :, span, 0:channels].reshape(near * WIN, channels)
            k = qkv[:, :, span, channels : 2 * channels].reshape(total * WIN, channels)
            v = qkv[:, :, span, 2 * channels :].reshape(total * WIN, channels)
            att = attend(
                (q * scale).astype(BF), k.astype(BF), v.astype(BF), same_token,
                masks_bf, masks_f32,
            )
            mixed[:, :, span, :] = att.reshape(2, members, WIN, channels)
        mixed_send[e] = mixed[1].astype(BF)
        backs.append(
            push(mixed_send.at[e], mixed_got.at[e], r_send.at[e], r_recv.at[e], mate)
        )

    def member_add(e, half, att):
        x = stream[e, half].reshape(members * part, channels)
        x = x + project(att.reshape(members * part, channels), mem_out[...])
        stream[e, half] = x.reshape(members, WIN // 2, WIN, channels)
        late[e, half] = normalize(x).reshape(members, part, channels)

    halo = []

    def send_halo(block, half):
        piece = late.at[block, half]
        toward = {"lat": lax.rem(lat + 2 * block - 1 + n_lat, n_lat)}
        for target, send, recv, peer in (
            (vert.at[1 - block, half], v_send.at[block, half], v_recv.at[1 - block, half], toward),
            (right.at[block, half], l_send.at[block, half], l_recv.at[block, half], lon_left),
            (left.at[block, half], rt_send.at[block, half], rt_recv.at[block, half], lon_right),
        ):
            halo.append(push(piece, target, send, recv, peer))

    def arrived(buffer, sem):
        pltpu.make_async_copy(buffer, buffer, sem).wait()

    for half in range(2):
        member_attention(half)
        member_add(core, half, mixed[0].astype(BF))
        send_halo(core, half)
    for half in range(2):
        arrived(mixed_got.at[half], r_recv.at[half])
        member_add(other, half, mixed_got[half])
        send_halo(other, half)

    mr, nr = row_low.astype(BF), (1.0 - row_low).astype(BF)
    mc, nc = col_low.astype(BF), (1.0 - col_low).astype(BF)

    def relay(half):
        arrived(vert.at[0, half], v_recv.at[0, half])
        arrived(vert.at[1, half], v_recv.at[1, half])
        h_tok = lax.broadcasted_iota(jnp.int32, (part, channels), 0) + half * part
        h_low = jnp.where(h_tok // WIN < split0, 1.0, 0.0)
        h_mr, h_nr = h_low.astype(BF), (1.0 - h_low).astype(BF)
        corner[half] = vert[0, half] * h_mr[None] + vert[1, half] * h_nr[None]
        halo.append(
            push(corner.at[half], corner_right.at[half], c_send.at[0, half],
                 c_recv.at[0, half], lon_left)
        )
        halo.append(
            push(corner.at[half], corner_left.at[half], c_send.at[1, half],
                 c_recv.at[1, half], lon_right)
        )

    relay(0)
    relay(1)

    q_tok = lax.broadcasted_iota(jnp.int32, (tokens, 4 * tokens), 0)
    k_tok = lax.broadcasted_iota(jnp.int32, (tokens, 4 * tokens), 1)
    q_row = jnp.where(q_tok // WIN < split0, 1, 0)
    q_col = jnp.where(lax.rem(q_tok, WIN) < split1, 1, 0)
    k_row = k_tok // (2 * tokens)
    k_col = lax.rem(k_tok // tokens, 2)
    k_low = jnp.where(lax.rem(k_tok, tokens) // WIN < split0, 1, 0)
    col_bias = jnp.where(q_col == k_col, 0.0, NEG)
    first = jnp.where(lat == 0, 1.0, 0.0)
    last = jnp.where(lat == n_lat - 1, 1.0, 0.0)
    outside = jnp.where(k_row == 0, jnp.where(k_low == 1, NEG, 0.0), 0.0) * first
    outside = outside + jnp.where(k_row == 1, jnp.where(k_low == 0, NEG, 0.0), 0.0) * last
    edge_bias = jnp.where(q_row == k_row, 0.0, NEG) + col_bias + outside
    inner_bias = col_bias[:, : 2 * tokens]

    for load in loads[7:]:
        load.wait()

    def whole(ref, m):
        return ref[:, m].reshape(tokens, channels)

    def joined(ref, e, m):
        return whole(ref.at[1 - e], m) * mr + whole(ref.at[e], m) * nr

    def stacked(pieces):
        return jnp.concatenate(pieces, axis=0)

    def ask(owns):
        return (project(stacked(owns), shift_qkv[:, :channels]) * scale).astype(BF)

    def to_keyed(pieces):
        return project(stacked(pieces), shift_qkv[:, channels:]).astype(BF)

    def residual(e):
        return stacked(
            [
                jnp.where(
                    is_low,
                    stream[1 - e, :, m].reshape(tokens, channels),
                    stream[e, :, m].reshape(tokens, channels),
                )
                for m in range(members)
            ]
        )

    def finish(e, x, asked, keyed, bias):
        atts = []
        for m in range(members):
            atts.append(
                attend(
                    asked[m * tokens : (m + 1) * tokens], keyed[m][:, :channels],
                    keyed[m][:, channels:], bias, masks_bf, masks_f32,
                )
            )
        x = x + project(stacked(atts).astype(BF), shift_out[...])
        x = feed_forward(x, shift_up[...], shift_down[...])
        for m in range(members):
            final[e, :, m] = x[m * tokens : (m + 1) * tokens].reshape(
                2, WIN // 2, WIN, channels
            )

    for block in range(2):
        for half in range(2):
            arrived(right.at[block, half], l_recv.at[block, half])
            arrived(left.at[block, half], rt_recv.at[block, half])
    owns = [joined(late, inner, m) for m in range(members)]
    windows = []
    for m in range(members):
        windows.append(joined(left, inner, m) * mc + owns[m] * nc)
        windows.append(owns[m] * mc + joined(right, inner, m) * nc)
    keyed = to_keyed(windows)
    keyed = [keyed[2 * m * tokens : 2 * (m + 1) * tokens] for m in range(members)]
    finish(inner, residual(inner), ask(owns), keyed, inner_bias)

    owns = [joined(late, edge, m) for m in range(members)]
    sides = [
        joined(left, edge, m) * mc + joined(right, edge, m) * nc for m in range(members)
    ]
    beyonds = [whole(corner, m) for m in range(members)]
    known = to_keyed(owns + sides + beyonds)
    edge_asked = ask(owns)
    edge_x = residual(edge)
    mr2, nr2 = [jnp.concatenate([mask, mask], axis=1) for mask in (mr, nr)]
    mc2, nc2 = [jnp.concatenate([mask, mask], axis=1) for mask in (mc, nc)]

    def piece_of(array, index):
        return array[index * tokens : (index + 1) * tokens]

    middles = []
    for m in range(members):
        own, beyond = piece_of(known, m), piece_of(known, 2 * members + m)
        middles.append((beyond * mr2 + own * nr2, own * mr2 + beyond * nr2))
    for half in range(2):
        arrived(corner_right.at[half], c_recv.at[0, half])
        arrived(corner_left.at[half], c_recv.at[1, half])
    fars = to_keyed(
        [whole(corner_left, m) * mc + whole(corner_right, m) * nc for m in range(members)]
    )
    keyed = []
    for m in range(members):
        side, far = piece_of(known, members + m), piece_of(fars, m)
        group = []
        for middle, flank in zip(
            middles[m], (far * mr2 + side * nr2, side * mr2 + far * nr2)
        ):
            group.append(flank * mc2 + middle * nc2)
            group.append(middle * mc2 + flank * nc2)
        keyed.append(stacked(group))
    finish(edge, edge_x, edge_asked, keyed, edge_bias)

    for b in range(2):
        spots = []
        for r in range(WIN):
            place = lax.rem(r + split0, WIN)
            low = jnp.where(place < split0, 1, 0)
            tile_of = low if b == 0 else 1 - low
            spots.append((tile_of, place // (WIN // 2), lax.rem(place, WIN // 2)))
        for m in range(members):
            tile = jnp.concatenate(
                [final[t, h, m, p].reshape(1, WIN, channels) for t, h, p in spots], axis=0
            )
            tile = pltpu.roll(tile, off1, 1)
            out[m, b * WIN : (b + 1) * WIN] = tile.astype(BF)

    for copy in list(sends.values()) + backs + halo:
        copy.wait_send()


def per_device(sizes, fields, land_mask, offsets, land_embed, *weights):
    members, height, breadth, channels = fields.shape
    tokens = WIN * WIN
    part = tokens // 2
    vmem = pl.BlockSpec(memory_space=pltpu.VMEM)
    hbm = pl.BlockSpec(memory_space=pltpu.HBM)
    piece = (members, part, channels)
    dma = pltpu.SemaphoreType.DMA
    scratch = [pltpu.VMEM(w.shape, w.dtype) for w in (fields,) + weights] + [
        pltpu.VMEM((2, 2, members, WIN // 2, WIN, channels), F32),
        pltpu.VMEM((2, 2) + piece, BF),
        pltpu.VMEM((3, 2) + piece, BF),
        pltpu.VMEM((4, members, part, 3 * channels), F32),
        pltpu.VMEM((2,) + piece, F32),
        pltpu.VMEM((2,) + piece, BF),
        pltpu.VMEM((2,) + piece, BF),
        pltpu.VMEM((2, 2) + piece, BF),
        pltpu.VMEM((2, 2) + piece, BF),
        pltpu.VMEM((2, 2) + piece, BF),
        pltpu.VMEM((2, 2) + piece, BF),
        pltpu.VMEM((2,) + piece, BF),
        pltpu.VMEM((2,) + piece, BF),
        pltpu.VMEM((2,) + piece, BF),
        pltpu.VMEM((2, 2, members, WIN // 2, WIN, channels), F32),
        dma((len(weights) + 1,)),
        dma((3, 2)), dma((3, 2)), dma((2,)), dma((2,)),
        dma((2, 2)), dma((2, 2)),
        dma((2, 2)), dma((2, 2)),
        dma((2, 2)), dma((2, 2)),
        dma((2, 2)), dma((2, 2)),
    ]
    return pl.pallas_call(
        functools.partial(kernel, sizes),
        out_shape=pltpu.VMEM(fields.shape, BF),
        in_specs=[hbm, vmem, pl.BlockSpec(memory_space=pltpu.SMEM), vmem]
        + [hbm] * len(weights),
        out_specs=vmem,
        scratch_shapes=scratch,
        compiler_params=pltpu.CompilerParams(collective_id=0, has_side_effects=True, vmem_limit_bytes=VMEM_LIMIT),
        name="scorer",
    )(fields, land_mask.T, offsets, land_embed.reshape(1, channels), *weights)


def solution(mesh):
    sizes = tuple(mesh.shape[axis] for axis in ("member", "lat", "lon"))
    return jax.shard_map(
        functools.partial(per_device, sizes),
        mesh=mesh,
        in_specs=(P("member", "lat", "lon", None), P("lat", "lon")) + (P(),) * 12,
        out_specs=P("member", "lat", "lon", None),
        check_vma=False,
    )
```

```python
import functools

import jax
import jax.numpy as jnp
from jax import lax
from jax.experimental import pallas as pl
from jax.experimental.pallas import tpu as pltpu
from jax.sharding import PartitionSpec as P

HEADS = 4
WIN = 8
EPS = 1e-05
VMEM_LIMIT = 58 * 1024 * 1024
NEG = -1e30
MESH = pl.DeviceIdType.MESH
BF = jnp.bfloat16
F32 = jnp.float32


def normalize(stream):
    average = jnp.mean(stream, axis=-1, keepdims=True)
    centered = stream - average
    spread = jnp.mean(centered * centered, axis=-1, keepdims=True)
    return (centered * lax.rsqrt(spread + EPS)).astype(BF)


def project(inputs, matrix):
    return jnp.dot(inputs, matrix, preferred_element_type=F32)


def gelu(x):
    return (0.5 * x) * (1.0 + lax.erf(x * 0.7071067811865476))


def feed_forward(stream, w_up, w_down):
    hidden = gelu(project(normalize(stream), w_up)).astype(BF)
    return stream + project(hidden, w_down)


def head_masks(channels, dtype):
    lane = lax.broadcasted_iota(jnp.int32, (1, channels), 1) // (channels // HEADS)
    return [jnp.where(lane == h, 1.0, 0.0).astype(dtype) for h in range(HEADS)]


def attend(q, k, v, bias, masks_bf, masks_f32):
    count = q.shape[0]
    stacked = jnp.concatenate([q * mask for mask in masks_bf], axis=0)
    scores = lax.dot_general(
        stacked, k, (((1,), (1,)), ((), ())), preferred_element_type=F32
    )
    if bias is not None:
        scores = (
            scores.reshape(HEADS, count, -1) + bias[None]
        ).reshape(scores.shape)
    top = jnp.max(scores, axis=-1, keepdims=True)
    weights = jnp.exp(scores - top)
    total = jnp.sum(weights, axis=-1, keepdims=True)
    weights = (weights * (1.0 / total)).astype(BF)
    wide = project(weights, v)
    result = wide[:count] * masks_f32[0]
    for h in range(1, HEADS):
        result = result + wide[h * count : (h + 1) * count] * masks_f32[h]
    return result


def kernel(
    sizes,
    h_fields, land, offsets, embed,
    h_win_qkv, h_win_out, h_win_up, h_win_down, h_mem_qkv, h_mem_out,
    h_shift_qkv, h_shift_out, h_shift_up, h_shift_down,
    out,
    fields, win_qkv, win_out, win_up, win_down, mem_qkv, mem_out,
    shift_qkv, shift_out, shift_up, shift_down,
    stream, mine, got, qkv, mixed, mixed_send, mixed_got,
    late, vert, left, right, corner, corner_left, corner_right, final,
    w_sem, a_send, a_recv, r_send, r_recv, v_send, v_recv,
    l_send, l_recv, rt_send, rt_recv, c_send, c_recv,
):
    n_member, n_lat, n_lon = sizes
    members = h_fields.shape[0]
    channels = h_fields.shape[-1]
    tokens = WIN * WIN
    part = tokens // 2
    edge, inner = 0, 1
    me = lax.axis_index("member")
    lat = lax.axis_index("lat")
    lon = lax.axis_index("lon")
    core = lax.rem(me, 2)
    chip = me // 2
    other = 1 - core
    mate = {"member": 2 * chip + other}
    far_same = {"member": 2 * (1 - chip) + core}
    far_other = {"member": 2 * (1 - chip) + other}
    lat_up = {"lat": lax.rem(lat + n_lat - 1, n_lat)}
    lat_down = {"lat": lax.rem(lat + 1, n_lat)}
    lon_left = {"lon": lax.rem(lon + n_lon - 1, n_lon)}
    lon_right = {"lon": lax.rem(lon + 1, n_lon)}

    barrier = pltpu.get_barrier_semaphore()
    for peer in (mate, far_same, far_other, lat_up, lat_down, lon_left, lon_right):
        pl.semaphore_signal(barrier, inc=1, device_id=peer, device_id_type=MESH)

    pairs = [
        (h_fields, fields),
        (h_win_qkv, win_qkv), (h_win_out, win_out), (h_win_up, win_up),
        (h_win_down, win_down), (h_mem_qkv, mem_qkv), (h_mem_out, mem_out),
        (h_shift_qkv, shift_qkv), (h_shift_out, shift_out),
        (h_shift_up, shift_up), (h_shift_down, shift_down),
    ]
    loads = [
        pltpu.make_async_copy(source, target, w_sem.at[i])
        for i, (source, target) in enumerate(pairs)
    ]
    for load in loads:
        load.start()

    off0 = offsets[0]
    off1 = offsets[1]
    split0 = WIN - off0
    split1 = WIN - off1
    masks_bf = head_masks(channels, BF)
    masks_f32 = head_masks(channels, F32)
    scale = (channels // HEADS) ** -0.5

    def push(source, target, send, recv, peer):
        copy = pltpu.make_async_remote_copy(
            src_ref=source, dst_ref=target, send_sem=send, recv_sem=recv,
            device_id=peer, device_id_type=MESH,
        )
        copy.start()
        return copy

    token = lax.broadcasted_iota(jnp.int32, (tokens, channels), 0)
    is_low = token // WIN < split0
    row_low = jnp.where(is_low, 1.0, 0.0)
    col_low = jnp.where(lax.rem(token, WIN) < split1, 1.0, 0.0)

    flags = pltpu.roll(land[...].astype(F32), split1, 0)
    spread = jnp.concatenate([flags] * WIN, axis=0)
    s_row = lax.broadcasted_iota(jnp.int32, spread.shape, 0) // WIN
    s_lane = lax.broadcasted_iota(jnp.int32, spread.shape, 1)
    s_pick = lax.rem(s_row + off0, WIN)
    loads[0].wait()

    def window_section(block, waits):
        rows = [WIN * block + lax.rem(s + off0, WIN) for s in range(WIN)]
        picked = jnp.where(s_lane == WIN * block + s_pick, spread, 0.0)
        added = jnp.sum(picked, axis=-1, keepdims=True) * embed[...]
        tiles = []
        for m in range(members):
            tile = jnp.concatenate(
                [fields[m, r].astype(F32).reshape(1, WIN, channels) for r in rows], axis=0
            )
            tiles.append(pltpu.roll(tile, split1, 1).reshape(tokens, channels) + added)
        x = jnp.concatenate(tiles, axis=0)
        if waits:
            loads[1].wait()
        proj = project(normalize(x), win_qkv[...])
        atts = []
        for m in range(members):
            span = slice(m * tokens, (m + 1) * tokens)
            q = (proj[span, :channels] * scale).astype(BF)
            k = proj[span, channels : 2 * channels].astype(BF)
            v = proj[span, 2 * channels :].astype(BF)
            atts.append(attend(q, k, v, None, masks_bf, masks_f32))
        if waits:
            loads[2].wait()
        x = x + project(jnp.concatenate(atts, axis=0).astype(BF), win_out[...])
        if waits:
            loads[3].wait()
            loads[4].wait()
        x = feed_forward(x, win_up[...], win_down[...])
        normed = normalize(x)
        for m in range(members):
            for half in range(2):
                first = m * tokens + half * part
                span = slice(first, first + part)
                stream[block, half, m] = x[span].reshape(WIN // 2, WIN, channels)
                mine[block, half, m] = normed[span]

    sends = {}

    def send_members(block, i, peer):
        for half in range(2):
            sends[i, half] = push(
                mine.at[block, half], got.at[i, half], a_send.at[i, half],
                a_recv.at[i, half], peer,
            )

    window_section(other, True)
    pl.semaphore_wait(barrier, 7)
    send_members(other, 1, far_other)
    send_members(other, 0, mate)
    window_section(core, False)
    send_members(core, 2, far_same)
    loads[5].wait()
    loads[6].wait()

    near = 2 * members
    total = 4 * members
    qt = lax.rem(lax.broadcasted_iota(jnp.int32, (near * WIN, total * WIN), 0), WIN)
    kt = lax.rem(lax.broadcasted_iota(jnp.int32, (near * WIN, total * WIN), 1), WIN)
    same_token = jnp.where(qt == kt, 0.0, NEG)
    backs = []

    def member_qkv(source, x, with_q):
        weights = mem_qkv[...] if with_q else mem_qkv[:, channels:]
        first_col = 0 if with_q else channels
        qkv[source, :, :, first_col:] = project(
            x.reshape(members * part, channels), weights
        ).reshape(members, part, -1)

    def member_attention(e):
        member_qkv(0, mine[core, e], True)
        sends[0, e].wait_recv()
        member_qkv(1, got[0, e], True)
        for i in (1, 2):
            sends[i, e].wait_recv()
            member_qkv(i + 1, got[i, e], False)
        for group in range(part // WIN):
            span = slice(group * WIN, (group + 1) * WIN)
            q = qkv[0:2, :, span, 0:channels].reshape(near * WIN, channels)
            k = qkv[:, :, span, channels : 2 * channels].reshape(total * WIN, channels)
            v = qkv[:, :, span, 2 * channels :].reshape(total * WIN, channels)
            att = attend(
                (q * scale).astype(BF), k.astype(BF), v.astype(BF), same_token,
                masks_bf, masks_f32,
            )
            mixed[:, :, span, :] = att.reshape(2, members, WIN, channels)
        mixed_send[e] = mixed[1].astype(BF)
        backs.append(
            push(mixed_send.at[e], mixed_got.at[e], r_send.at[e], r_recv.at[e], mate)
        )

    def member_add(e, half, att):
        x = stream[e, half].reshape(members * part, channels)
        x = x + project(att.reshape(members * part, channels), mem_out[...])
        stream[e, half] = x.reshape(members, WIN // 2, WIN, channels)
        late[e, half] = normalize(x).reshape(members, part, channels)

    halo = []

    def send_halo(block, half):
        piece = late.at[block, half]
        toward = {"lat": lax.rem(lat + 2 * block - 1 + n_lat, n_lat)}
        for target, send, recv, peer in (
            (vert.at[1 - block, half], v_send.at[block, half], v_recv.at[1 - block, half], toward),
            (right.at[block, half], l_send.at[block, half], l_recv.at[block, half], lon_left),
            (left.at[block, half], rt_send.at[block, half], rt_recv.at[block, half], lon_right),
        ):
            halo.append(push(piece, target, send, recv, peer))

    def arrived(buffer, sem):
        pltpu.make_async_copy(buffer, buffer, sem).wait()

    kept = []
    for half in range(2):
        member_attention(half)
        kept.append(mixed[0].astype(BF))
    for half in range(2):
        member_add(core, half, kept[half])
        send_halo(core, half)
    for half in range(2):
        arrived(mixed_got.at[half], r_recv.at[half])
        member_add(other, half, mixed_got[half])
        send_halo(other, half)

    mr, nr = row_low.astype(BF), (1.0 - row_low).astype(BF)
    mc, nc = col_low.astype(BF), (1.0 - col_low).astype(BF)

    def relay(half):
        arrived(vert.at[0, half], v_recv.at[0, half])
        arrived(vert.at[1, half], v_recv.at[1, half])
        h_tok = lax.broadcasted_iota(jnp.int32, (part, channels), 0) + half * part
        h_low = jnp.where(h_tok // WIN < split0, 1.0, 0.0)
        h_mr, h_nr = h_low.astype(BF), (1.0 - h_low).astype(BF)
        corner[half] = vert[0, half] * h_mr[None] + vert[1, half] * h_nr[None]
        halo.append(
            push(corner.at[half], corner_right.at[half], c_send.at[0, half],
                 c_recv.at[0, half], lon_left)
        )
        halo.append(
            push(corner.at[half], corner_left.at[half], c_send.at[1, half],
                 c_recv.at[1, half], lon_right)
        )

    relay(0)
    relay(1)

    q_tok = lax.broadcasted_iota(jnp.int32, (tokens, 4 * tokens), 0)
    k_tok = lax.broadcasted_iota(jnp.int32, (tokens, 4 * tokens), 1)
    q_row = jnp.where(q_tok // WIN < split0, 1, 0)
    q_col = jnp.where(lax.rem(q_tok, WIN) < split1, 1, 0)
    k_row = k_tok // (2 * tokens)
    k_col = lax.rem(k_tok // tokens, 2)
    k_low = jnp.where(lax.rem(k_tok, tokens) // WIN < split0, 1, 0)
    col_bias = jnp.where(q_col == k_col, 0.0, NEG)
    first = jnp.where(lat == 0, 1.0, 0.0)
    last = jnp.where(lat == n_lat - 1, 1.0, 0.0)
    outside = jnp.where(k_row == 0, jnp.where(k_low == 1, NEG, 0.0), 0.0) * first
    outside = outside + jnp.where(k_row == 1, jnp.where(k_low == 0, NEG, 0.0), 0.0) * last
    edge_bias = jnp.where(q_row == k_row, 0.0, NEG) + col_bias + outside
    inner_bias = col_bias[:, : 2 * tokens]

    for load in loads[7:]:
        load.wait()

    def whole(ref, m):
        return ref[:, m].reshape(tokens, channels)

    def joined(ref, e, m):
        return whole(ref.at[1 - e], m) * mr + whole(ref.at[e], m) * nr

    def stacked(pieces):
        return jnp.concatenate(pieces, axis=0)

    def ask(owns):
        return (project(stacked(owns), shift_qkv[:, :channels]) * scale).astype(BF)

    def to_keyed(pieces):
        return project(stacked(pieces), shift_qkv[:, channels:]).astype(BF)

    def residual(e):
        return stacked(
            [
                jnp.where(
                    is_low,
                    stream[1 - e, :, m].reshape(tokens, channels),
                    stream[e, :, m].reshape(tokens, channels),
                )
                for m in range(members)
            ]
        )

    def finish(e, x, asked, keyed, bias):
        atts = []
        for m in range(members):
            atts.append(
                attend(
                    asked[m * tokens : (m + 1) * tokens], keyed[m][:, :channels],
                    keyed[m][:, channels:], bias, masks_bf, masks_f32,
                )
            )
        x = x + project(stacked(atts).astype(BF), shift_out[...])
        x = feed_forward(x, shift_up[...], shift_down[...])
        for m in range(members):
            final[e, :, m] = x[m * tokens : (m + 1) * tokens].reshape(
                2, WIN // 2, WIN, channels
            )

    for block in range(2):
        for half in range(2):
            arrived(right.at[block, half], l_recv.at[block, half])
            arrived(left.at[block, half], rt_recv.at[block, half])
    owns = [joined(late, inner, m) for m in range(members)]
    windows = []
    for m in range(members):
        windows.append(joined(left, inner, m) * mc + owns[m] * nc)
        windows.append(owns[m] * mc + joined(right, inner, m) * nc)
    keyed = to_keyed(windows)
    keyed = [keyed[2 * m * tokens : 2 * (m + 1) * tokens] for m in range(members)]
    finish(inner, residual(inner), ask(owns), keyed, inner_bias)

    owns = [joined(late, edge, m) for m in range(members)]
    sides = [
        joined(left, edge, m) * mc + joined(right, edge, m) * nc for m in range(members)
    ]
    beyonds = [whole(corner, m) for m in range(members)]
    known = to_keyed(owns + sides + beyonds)
    edge_asked = ask(owns)
    edge_x = residual(edge)
    mr2, nr2 = [jnp.concatenate([mask, mask], axis=1) for mask in (mr, nr)]
    mc2, nc2 = [jnp.concatenate([mask, mask], axis=1) for mask in (mc, nc)]

    def piece_of(array, index):
        return array[index * tokens : (index + 1) * tokens]

    middles = []
    for m in range(members):
        own, beyond = piece_of(known, m), piece_of(known, 2 * members + m)
        middles.append((beyond * mr2 + own * nr2, own * mr2 + beyond * nr2))
    for half in range(2):
        arrived(corner_right.at[half], c_recv.at[0, half])
        arrived(corner_left.at[half], c_recv.at[1, half])
    fars = to_keyed(
        [whole(corner_left, m) * mc + whole(corner_right, m) * nc for m in range(members)]
    )
    keyed = []
    for m in range(members):
        side, far = piece_of(known, members + m), piece_of(fars, m)
        group = []
        for middle, flank in zip(
            middles[m], (far * mr2 + side * nr2, side * mr2 + far * nr2)
        ):
            group.append(flank * mc2 + middle * nc2)
            group.append(middle * mc2 + flank * nc2)
        keyed.append(stacked(group))
    finish(edge, edge_x, edge_asked, keyed, edge_bias)

    for b in range(2):
        spots = []
        for r in range(WIN):
            place = lax.rem(r + split0, WIN)
            low = jnp.where(place < split0, 1, 0)
            tile_of = low if b == 0 else 1 - low
            spots.append((tile_of, place // (WIN // 2), lax.rem(place, WIN // 2)))
        for m in range(members):
            tile = jnp.concatenate(
                [final[t, h, m, p].reshape(1, WIN, channels) for t, h, p in spots], axis=0
            )
            tile = pltpu.roll(tile, off1, 1)
            out[m, b * WIN : (b + 1) * WIN] = tile.astype(BF)

    for copy in list(sends.values()) + backs + halo:
        copy.wait_send()


def per_device(sizes, fields, land_mask, offsets, land_embed, *weights):
    members, height, breadth, channels = fields.shape
    tokens = WIN * WIN
    part = tokens // 2
    vmem = pl.BlockSpec(memory_space=pltpu.VMEM)
    hbm = pl.BlockSpec(memory_space=pltpu.HBM)
    piece = (members, part, channels)
    dma = pltpu.SemaphoreType.DMA
    scratch = [pltpu.VMEM(w.shape, w.dtype) for w in (fields,) + weights] + [
        pltpu.VMEM((2, 2, members, WIN // 2, WIN, channels), F32),
        pltpu.VMEM((2, 2) + piece, BF),
        pltpu.VMEM((3, 2) + piece, BF),
        pltpu.VMEM((4, members, part, 3 * channels), F32),
        pltpu.VMEM((2,) + piece, F32),
        pltpu.VMEM((2,) + piece, BF),
        pltpu.VMEM((2,) + piece, BF),
        pltpu.VMEM((2, 2) + piece, BF),
        pltpu.VMEM((2, 2) + piece, BF),
        pltpu.VMEM((2, 2) + piece, BF),
        pltpu.VMEM((2, 2) + piece, BF),
        pltpu.VMEM((2,) + piece, BF),
        pltpu.VMEM((2,) + piece, BF),
        pltpu.VMEM((2,) + piece, BF),
        pltpu.VMEM((2, 2, members, WIN // 2, WIN, channels), F32),
        dma((len(weights) + 1,)),
        dma((3, 2)), dma((3, 2)), dma((2,)), dma((2,)),
        dma((2, 2)), dma((2, 2)),
        dma((2, 2)), dma((2, 2)),
        dma((2, 2)), dma((2, 2)),
        dma((2, 2)), dma((2, 2)),
    ]
    return pl.pallas_call(
        functools.partial(kernel, sizes),
        out_shape=pltpu.VMEM(fields.shape, BF),
        in_specs=[hbm, vmem, pl.BlockSpec(memory_space=pltpu.SMEM), vmem]
        + [hbm] * len(weights),
        out_specs=vmem,
        scratch_shapes=scratch,
        compiler_params=pltpu.CompilerParams(collective_id=0, has_side_effects=True, vmem_limit_bytes=VMEM_LIMIT),
        name="scorer",
    )(fields, land_mask.T, offsets, land_embed.reshape(1, channels), *weights)


def solution(mesh):
    sizes = tuple(mesh.shape[axis] for axis in ("member", "lat", "lon"))
    return jax.shard_map(
        functools.partial(per_device, sizes),
        mesh=mesh,
        in_specs=(P("member", "lat", "lon", None), P("lat", "lon")) + (P(),) * 12,
        out_specs=P("member", "lat", "lon", None),
        check_vma=False,
    )
```
